128 devices in a mesh: expert: 32 (over y, z, core), hidden: 4 (over x).
Axes of the slice: x: 4, y: 4, z: 4, core: 2. Of those that a mesh axis runs over, the one named last changes fastest.
Arguments:
- tokens: bfloat16 [4096, 2048], P('expert', 'hidden'), may hold values from -6 to 6
- cotangent: bfloat16 [4096, 2048], P('expert', 'hidden'), may hold values from -6 to 6
- gate_weight: bfloat16 [64, 2048, 1408], P('expert', 'hidden'), may hold values from -0.125 to 0.125
- up_weight: bfloat16 [64, 2048, 1408], P('expert', 'hidden'), may hold values from -0.125 to 0.125
- down_weight: bfloat16 [64, 2048, 1408], P('expert', 'hidden'), may hold values from -0.15625 to 0.15625
- routing: int32 [4096, 6], P('expert'), may hold values from 0 to 63, all different within a row; in each aligned block of 128 rows (0 to 127, 128 to 255, ...) at most 16 rows name the same one
- route_weight: float32 [4096, 6], P('expert'), may hold values from 0.05 to 1
- merge_source: int32 [16], replicated, may hold values from 2 to 61, as said below
- merge_target: int32 [16], replicated, may hold values from 0 to 63, as said below
- neuron_perm: int32 [16, 1408], replicated, may hold values from 0 to 1407, as said below
Outputs:
- mixed: bfloat16 [4096, 2048], P('expert', 'hidden')
- grad_gate: bfloat16 [64, 2048, 1408], P('expert', 'hidden')
- grad_up: bfloat16 [64, 2048, 1408], P('expert', 'hidden')
- grad_down: bfloat16 [64, 2048, 1408], P('expert', 'hidden')
The draws below stay inside these ranges and needn't reach their ends.
Inputs may be any that keep to these rules, and one draw needn't show every extreme that they name: `routing`: in each aligned block of 128 tokens no expert is named more than 16 times, a bound that some block reaches. `merge_source`: 16 distinct experts, always including expert 2 and expert 64 - 3; merge_source and merge_target together hold exactly one expert of each aligned group of 2 consecutive expert numbers. `merge_target`: distinct experts, none of them a source, always including expert 0 and expert 64 - 1; see merge_source. `neuron_perm`: each row is a permutation of 0 to 1407.
All inputs are finite; a program needn't handle non-finite values.
Results may differ from the reference program's by a relative error of at most 0.019.
Values may be sent and summed in bfloat16 or wider, within the bound.
A program may use at most 128 MiB of HBM per device.

```python
import math
import jax
import jax.numpy as jnp
import numpy as np
from jax import lax

D = 2048
FF = 1408
TOP = 6
EXP_DEV = 2
TOK_DEV = 128
EXPERTS = 64
TOKENS = 4096
MERGES = 16
MOST = 16
N_HIDDEN = 4


def pairing(key):
    holders = EXPERTS // EXP_DEV
    inner = (jax.random.permutation(jax.random.fold_in(key, 101), holders - 4) + 2).astype(jnp.int32)
    target_ends = jnp.array([0, holders - 1], dtype=jnp.int32)
    source_ends = jnp.array([1, holders - 2], dtype=jnp.int32)
    target_dev = jnp.concatenate([target_ends, inner[:MERGES - 2]])
    source_dev = jnp.concatenate([source_ends, inner[MERGES - 2:]])
    target_places = jax.random.randint(jax.random.fold_in(key, 202), (MERGES,), 0, EXP_DEV).astype(jnp.int32)
    target_places = target_places.at[0].set(0).at[1].set(EXP_DEV - 1)
    source_places = jax.random.randint(jax.random.fold_in(key, 404), (MERGES,), 0, EXP_DEV).astype(jnp.int32)
    source_places = source_places.at[0].set(0).at[1].set(EXP_DEV - 1)
    return ((source_dev * EXP_DEV + source_places).astype(jnp.int32), (target_dev * EXP_DEV + target_places).astype(jnp.int32))


def draw_merge_source(key, part):
    return pairing(key)[0]


def draw_merge_target(key, part):
    return pairing(key)[1]


def draw_neuron_perm(key, part):
    streams = jax.random.split(jax.random.fold_in(key, 303), MERGES)
    return jax.vmap(lambda stream: jax.random.permutation(stream, FF))(streams).astype(jnp.int32)


def steps_of(key, extent, cuts, least, largest):
    gain, own = 1.0, jax.random.fold_in(key, 6)
    for position, parts in cuts:
        draws = jnp.exp(jax.random.uniform(jax.random.fold_in(own, position), (parts,), jnp.float32, least / len(cuts), largest / len(cuts)))
        gain = gain * jnp.repeat(draws, extent[position] // parts).reshape([-1 if axis == position else 1 for axis in range(len(extent))])
    return gain


def deal_out(key, own, number, rows, amount, top, bound, skew):
    order = jax.random.permutation(key, amount)
    crowded, common = shares(amount, rows * top, bound, skew, True), shares(amount, rows * top, bound, skew, False)
    places = jnp.arange(amount)

    def named(tallies, turn):
        used = int((tallies > 0).sum())
        fixed = max(1, used // 4)
        passed = fixed + (places - fixed + turn * (used - fixed)) % max(1, amount - fixed)
        return jnp.zeros((amount,), jnp.int32).at[order[jnp.where(places < fixed, places, passed)]].set(jnp.asarray(tallies, jnp.int32))

    tallies = jnp.where(number % 4 == 0, named(crowded, number // 4), named(common, number - number // 4 - 1))
    mixed = jax.random.permutation(jax.random.fold_in(own, 3), amount)
    source_of, receiver = mixed[0:amount // 2 * 2:2], mixed[1:amount // 2 * 2:2]
    margin = jnp.minimum(tallies[source_of] - 1, bound - tallies[receiver]) // 2
    margin = jnp.where((source_of == order[0]) | (receiver == order[0]) | (tallies[receiver] == 0), 0, jnp.maximum(margin, 0))
    passed = jax.random.randint(jax.random.fold_in(own, 4), (amount // 2,), 0, 1 << 20) % (margin + 1)
    tallies = tallies.at[source_of].add(-passed).at[receiver].add(passed)
    members = jnp.searchsorted(jnp.cumsum(tallies), jnp.arange(rows * top), side="right").astype(jnp.int32)
    listing = members.reshape(top, rows).T
    listing = listing[jax.random.permutation(jax.random.fold_in(own, 1), rows)]
    turn = jax.random.randint(jax.random.fold_in(own, 2), (rows, 1), 0, top)
    return jnp.take_along_axis(listing, (jnp.arange(top)[None, :] + turn) % top, axis=1)


def shares(count, total, limit, skew, full):
    weights = [(1 << 20) // math.isqrt(grade ** skew) + 1 for grade in range(1, count + 1)]
    largest = limit if full else min(limit, max(-(-total // count), total * weights[0] // sum(weights)))
    least = 1 if total - largest >= count - 1 else 0
    given, rest = [largest] + [least] * (count - 1), total - largest - least * (count - 1)
    while rest > 0:
        candidates = [i for i in range(1, count) if given[i] < largest] or [i for i in range(1, count) if given[i] < limit]
        pool, remaining = sum([weights[i] for i in candidates]), rest
        for i in candidates:
            more = min(limit - given[i], max(1, remaining * weights[i] // pool), rest)
            given[i] = given[i] + more
            rest = rest - more
    return np.array(given)


def noise(own_key, shape, width, limit, shards=(), held_as=jnp.bfloat16):
    entries = jax.random.normal(own_key, shape, jnp.float32) * width
    if len(shards) > 0:
        entries = steps_of(own_key, shape, shards, -0.22, 0.18) * entries
    return jnp.clip(entries, min=-limit, max=limit).astype(held_as)


def setup_inputs(seed: int = 0) -> dict:
    streams_of = jax.random.split(jax.random.key(seed), 11)
    tokens = noise(streams_of[0], (TOKENS, D), 1.0, 6.0, ((0, 32), (1, 4)))
    cotangent = noise(streams_of[1], (TOKENS, D), 1.0, 6.0, ((0, 32), (1, 4)))
    gate_weight = noise(streams_of[2], (EXPERTS, D, FF), D ** -0.5, 0.125, ((0, 32), (1, 4)))
    up_weight = noise(streams_of[3], (EXPERTS, D, FF), D ** -0.5, 0.125, ((0, 32), (1, 4)))
    down_weight = noise(streams_of[4], (EXPERTS, D, FF), FF ** -0.5, 0.15625, ((0, 32), (1, 4)))
    routing_keys = jax.random.split(jax.random.fold_in(streams_of[5], 1), TOKENS // TOK_DEV)
    routing_turns = jax.random.permutation(jax.random.fold_in(streams_of[5], 3), TOKENS // TOK_DEV)
    routing = jax.vmap(lambda own, number: deal_out(jax.random.fold_in(streams_of[5], 2), own, number, TOK_DEV, EXPERTS, TOP, MOST, 2))(routing_keys, routing_turns).reshape((TOKENS, TOP))
    route_weight = jnp.clip(0.05 + 0.95 * jax.random.uniform(streams_of[6], (TOKENS, TOP), jnp.float32) ** steps_of(streams_of[6], (TOKENS, TOP), ((0, 32),), -0.2, 0.2), 0.05, 1.0)
    merge_source = draw_merge_source(jax.random.fold_in(streams_of[10], 71), 0)
    merge_target = draw_merge_target(jax.random.fold_in(streams_of[10], 71), 0)
    neuron_perm = draw_neuron_perm(jax.random.fold_in(streams_of[10], 71), 0)
    return dict(tokens=tokens, cotangent=cotangent, gate_weight=gate_weight, up_weight=up_weight, down_weight=down_weight, routing=routing, route_weight=route_weight, merge_source=merge_source, merge_target=merge_target, neuron_perm=neuron_perm)


def silu_parts(values):
    sigma = jax.nn.sigmoid(values)
    return values * sigma, sigma * (1.0 + values * (1.0 - sigma))


def shard_sums(activ, weight, group_n, row_count):
    left = activ.astype(jnp.float32).reshape(group_n, row_count, N_HIDDEN, D // N_HIDDEN)
    right = weight.astype(jnp.float32).reshape(group_n, N_HIDDEN, D // N_HIDDEN, FF)
    pieces = jnp.einsum('grhd,ghdf->ghrf', left, right)
    pieces = lax.optimization_barrier(pieces.astype(jnp.bfloat16))
    return jnp.sum(pieces.astype(jnp.float32), axis=1)


def merge_weight(weight, merge_source, merge_target, neuron_perm):
    moved = jax.vmap(lambda block, order: block[:, order])(weight[merge_source], neuron_perm)
    blended = (0.5 * (weight[merge_target].astype(jnp.float32) + moved.astype(jnp.float32))).astype(jnp.bfloat16)
    return weight.at[merge_target].set(blended)


def reference(tokens, cotangent, gate_weight, up_weight, down_weight, routing, route_weight, merge_source, merge_target, neuron_perm):
    devices_n = EXPERTS // EXP_DEV
    groups = EXP_DEV + 1
    row_count = devices_n * MOST
    slot_total = devices_n * groups * row_count
    assign_n = TOKENS * TOP
    expert_ids = jnp.arange(EXPERTS, dtype=jnp.int32)
    source_hit = merge_source[:, None] == expert_ids[None, :]
    is_source = jnp.any(source_hit, axis=0)
    mapped = jnp.where(is_source, jnp.sum(jnp.where(source_hit, merge_target[:, None], 0), axis=0), expert_ids).astype(jnp.int32)
    group_of = jnp.where(is_source, EXP_DEV, mapped % EXP_DEV).astype(jnp.int32)
    flat_ids = routing.reshape(-1).astype(jnp.int32)
    expert_hot = (flat_ids[:, None] == expert_ids[None, :]).astype(jnp.int32).reshape(devices_n, TOK_DEV * TOP, EXPERTS)
    rank_in = (jnp.sum(jnp.cumsum(expert_hot, axis=1) * expert_hot, axis=2) - 1).reshape(-1).astype(jnp.int32)
    block_of = (jnp.arange(assign_n, dtype=jnp.int32) // (TOK_DEV * TOP)).astype(jnp.int32)
    slot_index = ((mapped[flat_ids] // EXP_DEV) * (groups * row_count) + group_of[flat_ids] * row_count + block_of * MOST + rank_in).astype(jnp.int32)
    token_of = (jnp.arange(assign_n, dtype=jnp.int32) // TOP).astype(jnp.int32)
    weight_flat = route_weight.reshape(-1)
    slot_x = jnp.zeros((slot_total, D), jnp.bfloat16).at[slot_index].set(tokens[token_of])
    scaled = (weight_flat[:, None] * cotangent[token_of].astype(jnp.float32)).astype(jnp.bfloat16)
    slot_dy = jnp.zeros((slot_total, D), jnp.bfloat16).at[slot_index].set(scaled)

    merged_gate = merge_weight(gate_weight, merge_source, merge_target, neuron_perm).reshape(devices_n, EXP_DEV, D, FF)
    merged_up = merge_weight(up_weight, merge_source, merge_target, neuron_perm).reshape(devices_n, EXP_DEV, D, FF)
    merged_down = merge_weight(down_weight, merge_source, merge_target, neuron_perm).reshape(devices_n, EXP_DEV, D, FF)
    target_dev = merge_target // EXP_DEV
    pair_hit = target_dev[:, None] == jnp.arange(devices_n, dtype=jnp.int32)[None, :]
    target_slot = jnp.sum(jnp.where(pair_hit, (merge_target % EXP_DEV)[:, None], 0), axis=0).astype(jnp.int32)

    def per_device(packed):
        w_gate, w_up, w_down, slot_k, inputs_x, inputs_dy = packed

        def widen(weight):
            chosen = lax.dynamic_index_in_dim(weight, slot_k, 0, keepdims=True)
            return jnp.concatenate([weight, chosen], axis=0)

        w_gate, w_up, w_down = widen(w_gate), widen(w_up), widen(w_down)
        gate_sum = shard_sums(inputs_x, w_gate, groups, row_count)
        up_sum = shard_sums(inputs_x, w_up, groups, row_count)
        active, slope = silu_parts(gate_sum)
        hidden_act = (active * up_sum).astype(jnp.bfloat16)
        outputs_y = jnp.einsum('grf,gdf->grd', hidden_act.astype(jnp.float32), w_down.astype(jnp.float32)).astype(jnp.bfloat16)
        grad_down = jnp.einsum('grd,grf->gdf', inputs_dy.astype(jnp.float32), hidden_act.astype(jnp.float32))
        back_sum = shard_sums(inputs_dy, w_down, groups, row_count)
        grad_gate_act = (back_sum * up_sum * slope).astype(jnp.bfloat16)
        grad_up_act = (back_sum * active).astype(jnp.bfloat16)
        grad_gate = jnp.einsum('grd,grf->gdf', inputs_x.astype(jnp.float32), grad_gate_act.astype(jnp.float32))
        grad_up = jnp.einsum('grd,grf->gdf', inputs_x.astype(jnp.float32), grad_up_act.astype(jnp.float32))

        def fold(grad):
            base = grad[:EXP_DEV]
            extra = lax.dynamic_index_in_dim(base, slot_k, 0, keepdims=False) + grad[EXP_DEV]
            return lax.dynamic_update_index_in_dim(base, extra, slot_k, 0).astype(jnp.bfloat16)

        return outputs_y, fold(grad_gate), fold(grad_up), fold(grad_down)

    packed = (merged_gate, merged_up, merged_down, target_slot,
              slot_x.reshape(devices_n, groups, row_count, D), slot_dy.reshape(devices_n, groups, row_count, D))
    outputs_y, grad_gate, grad_up, grad_down = lax.map(per_device, packed)
    gathered = outputs_y.reshape(slot_total, D)[slot_index].astype(jnp.float32) * weight_flat[:, None]
    mixed = jnp.sum(gathered.reshape(TOKENS, TOP, D), axis=1).astype(jnp.bfloat16)
    return (mixed, grad_gate.reshape(EXPERTS, D, FF), grad_up.reshape(EXPERTS, D, FF), grad_down.reshape(EXPERTS, D, FF))
```

```python
import jax
import jax.numpy as jnp
from jax import lax
from jax.sharding import PartitionSpec as P

BF = jnp.bfloat16
F32 = jnp.float32


def silu_parts(values):
    sigma = jax.nn.sigmoid(values)
    return (values * sigma, sigma * (1.0 + values * (1.0 - sigma)))


def mm(a, b):
    return jnp.dot(a, b, preferred_element_type=F32)


def mm_nt(a, b):
    return lax.dot_general(a, b, (((1,), (1,)), ((), ())), preferred_element_type=F32)


def mm_tn(a, b):
    return lax.dot_general(a, b, (((0,), (0,)), ((), ())), preferred_element_type=F32)


def exchange(values):
    return lax.all_to_all(values, "expert", split_axis=0, concat_axis=0, tiled=True)


def reduced(part):
    return lax.psum_scatter(part.astype(BF), "hidden", scatter_dimension=0, tiled=True).astype(F32)


def spread(values):
    return lax.all_gather(values, "hidden", axis=0, tiled=True)


def shards(
    tokens,
    cotangent,
    gate_weight,
    up_weight,
    down_weight,
    routing,
    route_weight,
    merge_source,
    merge_target,
    neuron_perm,
):
    devices_n = lax.axis_size("expert")
    me = lax.axis_index("expert")
    exp_local, width, neurons = gate_weight.shape
    experts = exp_local * devices_n
    half = neurons // 2
    tok_local, top_count = routing.shape
    depth = max(2, tok_local * top_count * 4 // (3 * experts))
    expert_ids = jnp.arange(experts, dtype=jnp.int32)
    device_ids = jnp.arange(devices_n, dtype=jnp.int32)

    src_hit = (merge_source[:, None] // exp_local) == device_ids[None, :]
    tgt_hit = (merge_target[:, None] // exp_local) == device_ids[None, :]
    any_hit = src_hit | tgt_hit

    def pick(hit, values):
        return jnp.sum(jnp.where(hit, values[:, None], 0), axis=0)

    source_of = pick(any_hit, merge_source)
    target_of = pick(any_hit, merge_target)
    is_src = jnp.any(src_hit, axis=0)
    own_merge = jnp.where(is_src, source_of, target_of)
    partner_dev = jnp.where(is_src, target_of, source_of) // exp_local
    plain_of = device_ids * exp_local * 2 + (exp_local - 1) - own_merge
    i_am_src = jnp.any((merge_source // exp_local) == me)
    merge_slot = jnp.sum(jnp.where(device_ids == me, own_merge, 0)) - me * exp_local
    plain_slot = 1 - merge_slot

    mine = ((merge_source // exp_local) == me) | ((merge_target // exp_local) == me)
    perm = jnp.sum(jnp.where(mine[:, None], neuron_perm, 0), axis=0)
    order = jnp.where(i_am_src, perm, jnp.arange(neurons, dtype=jnp.int32))
    hot = (order[None, :] == jnp.arange(neurons, dtype=jnp.int32)[:, None]).astype(BF)

    def one(weight, slot):
        return lax.dynamic_index_in_dim(weight, slot, 0, keepdims=False)

    stack = jnp.concatenate([one(w, merge_slot) for w in (gate_weight, up_weight, down_weight)], 0)
    ordered = mm(stack, hot).astype(BF)
    first, second = ordered[:, :half], ordered[:, half:]
    keep = jnp.where(i_am_src, second, first)
    send = jnp.where(i_am_src, first, second)

    def relay(values):
        rows, cols = values.shape
        there = exchange(values.reshape(devices_n, rows // devices_n, cols))
        there = jnp.take(there, partner_dev, axis=0)
        return exchange(there).reshape(rows, cols)

    got = relay(send)
    blended = (0.5 * (keep.astype(F32) + got.astype(F32))).astype(BF)
    merged = blended.reshape(3, width, half)

    slot_expert = jnp.stack([plain_of, target_of, source_of], axis=1).reshape(-1)
    hit = routing.T[None, :, :] == slot_expert[:, None, None]
    chosen = jnp.any(hit, axis=1)
    chosen_w = jnp.sum(jnp.where(hit, route_weight.T[None, :, :], 0.0), axis=1)
    tok_ids = jnp.arange(tok_local, dtype=jnp.int32)
    before = (tok_ids[:, None] < tok_ids[None, :]).astype(BF)
    rank = mm(chosen.astype(BF), before).astype(jnp.int32)
    rank = jnp.where(chosen, rank, -1)
    place = rank[:, None, :] == jnp.arange(depth, dtype=jnp.int32)[None, :, None]
    slot_w = jnp.sum(jnp.where(place, chosen_w[:, None, :], 0.0), axis=2)
    place = place.astype(BF).reshape(devices_n, 3, depth, tok_local)
    slot_w = slot_w.reshape(devices_n, 3, depth)
    place_p = place[:, 0].reshape(-1, tok_local)
    place_m = place[:, 1:].reshape(-1, tok_local)
    w_p = slot_w[:, 0].reshape(-1)
    w_m = slot_w[:, 1:].reshape(-1)

    def dispatch(place, weights):
        rows = place.shape[0]
        x = mm(place, tokens).astype(BF).reshape(devices_n, rows // devices_n, width)
        dy = (mm(place, cotangent) * weights[:, None]).astype(BF)
        dy = dy.reshape(devices_n, rows // devices_n, width)
        return exchange(x).reshape(rows, width), exchange(dy).reshape(rows, width)

    x_p, dy_p = dispatch(place_p, w_p)
    x_m, dy_m = dispatch(place_m, w_m)

    def partials(x, dy, gate, up, down):
        return reduced(mm(x, gate)), reduced(mm(x, up)), reduced(mm(dy, down))

    def acts(g, u, dh):
        active, slope = silu_parts(g)
        h = (active * u).astype(BF)
        dg = (dh * u * slope).astype(BF)
        du = (dh * active).astype(BF)
        return spread(h), spread(dg), spread(du)

    plain_w = [one(w, plain_slot) for w in (gate_weight, up_weight, down_weight)]
    sums_p = partials(x_p, dy_p, *plain_w)
    sums_m = partials(x_m, dy_m, merged[0], merged[1], merged[2])
    h_m, dg_m, du_m = acts(*sums_m)
    h_p, dg_p, du_p = acts(*sums_p)

    def grads(x, dy, h, dg, du):
        return [mm_tn(x, dg).astype(BF), mm_tn(x, du).astype(BF), mm_tn(dy, h).astype(BF)]

    grads_m = jnp.concatenate(grads(x_m, dy_m, h_m, dg_m, du_m), axis=0)
    far = relay(grads_m)
    y_m = mm_nt(h_m, merged[2]).astype(BF)
    back_m = exchange(y_m.reshape(devices_n, -1, width)).reshape(-1, width)
    y_p = mm_nt(h_p, plain_w[2]).astype(BF)
    back_p = exchange(y_p.reshape(devices_n, -1, width)).reshape(-1, width)
    grads_p = grads(x_p, dy_p, h_p, dg_p, du_p)

    def combine(place, weights, back):
        hi = weights.astype(BF)
        lo = (weights - hi.astype(F32)).astype(BF)
        return mm_tn(place * hi[:, None], back) + mm_tn(place * lo[:, None], back)

    mixed = (combine(place_p, w_p, back_p) + combine(place_m, w_m, back_m)).astype(BF)

    outs = []
    for index, plain in enumerate(grads_p):
        rows = slice(index * width, (index + 1) * width)
        full = jnp.concatenate([grads_m[rows], far[rows]], axis=1)
        full = jnp.where(i_am_src, jnp.zeros_like(full), full)
        first_is_merge = merge_slot == 0
        outs.append(
            jnp.stack([jnp.where(first_is_merge, full, plain), jnp.where(first_is_merge, plain, full)])
        )
    return (mixed, *outs)


def solution(mesh):
    placed = (
        P("expert", "hidden"),
        P("expert", "hidden"),
        P("expert", "hidden", None),
        P("expert", "hidden", None),
        P("expert", "hidden", None),
        P("expert", None),
        P("expert", None),
        P(),
        P(),
        P(),
    )
    return jax.shard_map(
        shards,
        mesh=mesh,
        in_specs=placed,
        out_specs=(
            P("expert", "hidden"),
            P("expert", "hidden", None),
            P("expert", "hidden", None),
            P("expert", "hidden", None),
        ),
        check_vma=False,
    )
```

```python
import jax
import jax.numpy as jnp
from jax import lax
from jax.experimental import pallas as pl
from jax.experimental.pallas import tpu as pltpu
from jax.sharding import PartitionSpec as P

BF = jnp.bfloat16
F32 = jnp.float32
MESH = pl.DeviceIdType.MESH


def silu_parts(values):
    sigma = jax.nn.sigmoid(values)
    return (values * sigma, sigma * (1.0 + values * (1.0 - sigma)))


def mm(a, b):
    return jnp.dot(a, b, preferred_element_type=F32)


def mm_nt(a, b):
    return lax.dot_general(a, b, (((1,), (1,)), ((), ())), preferred_element_type=F32)


def mm_tn(a, b):
    return lax.dot_general(a, b, (((0,), (0,)), ((), ())), preferred_element_type=F32)


def exchange(values):
    return lax.all_to_all(values, "expert", split_axis=0, concat_axis=0, tiled=True)


def add_to(ref, other):
    ref[...] = (ref[...].astype(F32) + other[...].astype(F32)).astype(BF)


def hidden_kernel(
    x_ref, dy_ref, gate_ref, up_ref, down_ref, cover_ref, full, part, in_a, in_b, in_l, in_r, own, sends, recvs
):
    n = 4
    me = lax.axis_index("hidden")
    right, left, across = lax.rem(me + 1, n), lax.rem(me + 3, n), lax.rem(me + 2, n)
    chunk = part.shape[2]
    half = chunk // 2

    barrier = pltpu.get_barrier_semaphore()
    for peer in (left, right):
        pl.semaphore_signal(barrier, inc=1, device_id={"hidden": peer}, device_id_type=MESH)
    pl.semaphore_wait(barrier, 2)

    def send(src, dst, kind, q, peer):
        copy = pltpu.make_async_remote_copy(
            src_ref=src,
            dst_ref=dst,
            send_sem=sends.at[kind, q],
            recv_sem=recvs.at[kind, q],
            device_id={"hidden": peer},
            device_id_type=MESH,
        )
        copy.start()
        return copy

    pairs = ((x_ref, gate_ref), (x_ref, up_ref), (dy_ref, down_ref))

    def product(q, index):
        rows, weight = pairs[q]
        return mm(rows[pl.ds(pl.multiple_of(index * chunk, chunk), chunk), :], weight[...])

    first, second = pl.ds(0, half), pl.ds(half, half)
    step1, step2, step3, step4 = [], [], [], []
    for q in range(3):
        part[q, across] = product(q, across).astype(BF)
        step1.append(
            (
                send(part.at[q, across, first], in_a.at[q], 0, q, right),
                send(part.at[q, across, second], in_b.at[q], 1, q, left),
            )
        )
    for q in range(3):
        part[q, right] = product(q, right).astype(BF)
        part[q, left] = product(q, left).astype(BF)
        step1[q][0].wait_recv()
        add_to(part.at[q, right, first], in_a.at[q])
        a = send(part.at[q, right], in_l.at[q], 2, q, right)
        step1[q][1].wait_recv()
        add_to(part.at[q, left, second], in_b.at[q])
        step2.append((a, send(part.at[q, left], in_r.at[q], 3, q, left)))
    for q in range(3):
        own[q] = product(q, me)

    def total(q):
        step2[q][0].wait_recv()
        step2[q][1].wait_recv()
        return own[q].astype(BF).astype(F32) + in_l[q].astype(F32) + in_r[q].astype(F32)

    cover = cover_ref[0:1, :]

    def publish(q, value):
        full[q, me] = (value * cover).astype(BF)
        step3.append(
            (
                send(full.at[q, me], full.at[q, me], 4, q, right),
                send(full.at[q, me], full.at[q, me], 5, q, left),
            )
        )

    g = total(0)
    u = total(1)
    active, slope = silu_parts(g)
    publish(0, active * u)
    own[0] = active
    own[1] = u * slope
    dh = total(2)
    publish(1, dh * own[1])
    publish(2, dh * own[0])
    for q in range(3):
        step3[q][0].wait_recv()
        a = send(full.at[q, left, first], full.at[q, left, first], 6, q, right)
        step3[q][1].wait_recv()
        step4.append((a, send(full.at[q, right, second], full.at[q, right, second], 7, q, left)))
    for q in range(3):
        for copy in step4[q]:
            copy.wait_recv()
    for step in (step1, step2, step3, step4):
        for copies in step:
            for copy in copies:
                copy.wait_send()


def hidden_block(x, dy, gate, up, down, cover, ident):
    rows, cols = x.shape[0], gate.shape[1]
    chunk = rows // 4
    vmem = pl.BlockSpec(memory_space=pltpu.VMEM)
    full = pl.pallas_call(
        hidden_kernel,
        out_shape=jax.ShapeDtypeStruct((3, 4, chunk, cols), BF),
        in_specs=[vmem] * 6,
        out_specs=vmem,
        scratch_shapes=[
            pltpu.VMEM((3, 4, chunk, cols), BF),
            pltpu.VMEM((3, chunk // 2, cols), BF),
            pltpu.VMEM((3, chunk // 2, cols), BF),
            pltpu.VMEM((3, chunk, cols), BF),
            pltpu.VMEM((3, chunk, cols), BF),
            pltpu.VMEM((3, chunk, cols), F32),
            pltpu.SemaphoreType.DMA((8, 3)),
            pltpu.SemaphoreType.DMA((8, 3)),
        ],
        compiler_params=pltpu.CompilerParams(
            collective_id=ident, has_side_effects=True, vmem_limit_bytes=56 * 1024 * 1024
        ),
        cost_estimate=pl.CostEstimate(flops=60_000_000_000, bytes_accessed=200_000_000, transcendentals=0),
    )(x, dy, gate, up, down, cover)
    return [full[q].reshape(rows, cols) for q in range(3)]


def shards(
    tokens,
    cotangent,
    gate_weight,
    up_weight,
    down_weight,
    routing,
    route_weight,
    merge_source,
    merge_target,
    neuron_perm,
):
    devices_n = lax.axis_size("expert")
    me = lax.axis_index("expert")
    exp_local, width, neurons = gate_weight.shape
    experts = exp_local * devices_n
    half = -(-neurons // 256) * 128
    tail = neurons - half
    tok_local, top_count = routing.shape
    depth = max(2, tok_local * top_count * 4 // (3 * experts))
    expert_ids = jnp.arange(experts, dtype=jnp.int32)
    device_ids = jnp.arange(devices_n, dtype=jnp.int32)

    src_hit = (merge_source[:, None] // exp_local) == device_ids[None, :]
    tgt_hit = (merge_target[:, None] // exp_local) == device_ids[None, :]
    any_hit = src_hit | tgt_hit

    def pick(hit, values):
        return jnp.sum(jnp.where(hit, values[:, None], 0), axis=0)

    source_of = pick(any_hit, merge_source)
    target_of = pick(any_hit, merge_target)
    is_src = jnp.any(src_hit, axis=0)
    own_merge = jnp.where(is_src, source_of, target_of)
    partner_dev = jnp.where(is_src, target_of, source_of) // exp_local
    plain_of = device_ids * exp_local * 2 + (exp_local - 1) - own_merge
    i_am_src = jnp.any((merge_source // exp_local) == me)
    merge_slot = jnp.sum(jnp.where(device_ids == me, own_merge, 0)) - me * exp_local
    plain_slot = 1 - merge_slot

    mine = ((merge_source // exp_local) == me) | ((merge_target // exp_local) == me)
    perm = jnp.sum(jnp.where(mine[:, None], neuron_perm, 0), axis=0)
    order = jnp.where(i_am_src, perm, jnp.arange(neurons, dtype=jnp.int32))
    hot = (order[None, :] == jnp.arange(neurons, dtype=jnp.int32)[:, None]).astype(BF)

    def one(weight, slot):
        return lax.dynamic_index_in_dim(weight, slot, 0, keepdims=False)

    stack = jnp.concatenate([one(w, merge_slot) for w in (gate_weight, up_weight, down_weight)], 0)
    ordered = mm(stack, hot).astype(BF)
    first, second = ordered[:, :half], ordered[:, tail:]
    keep = jnp.where(i_am_src, second, first)
    send = jnp.where(i_am_src, first, second)

    def relay(values):
        rows, cols = values.shape
        there = exchange(values.reshape(devices_n, rows // devices_n, cols))
        there = jnp.take(there, partner_dev, axis=0)
        return exchange(there).reshape(rows, cols)

    got = relay(send)
    blended = (0.5 * (keep.astype(F32) + got.astype(F32))).astype(BF)
    merged = blended.reshape(3, width, half)

    slot_expert = jnp.stack([plain_of, target_of, source_of], axis=1).reshape(-1)
    hit = routing.T[None, :, :] == slot_expert[:, None, None]
    chosen = jnp.any(hit, axis=1)
    chosen_w = jnp.sum(jnp.where(hit, route_weight.T[None, :, :], 0.0), axis=1)
    tok_ids = jnp.arange(tok_local, dtype=jnp.int32)
    before = (tok_ids[:, None] < tok_ids[None, :]).astype(BF)
    rank = mm(chosen.astype(BF), before).astype(jnp.int32)
    rank = jnp.where(chosen, rank, -1)
    place = rank[:, None, :] == jnp.arange(depth, dtype=jnp.int32)[None, :, None]
    slot_w = jnp.sum(jnp.where(place, chosen_w[:, None, :], 0.0), axis=2)
    place = place.astype(BF).reshape(devices_n, 3, depth, tok_local)
    slot_w = slot_w.reshape(devices_n, 3, depth)
    place_p = place[:, 0].reshape(-1, tok_local)
    place_m = place[:, 1:].reshape(-1, tok_local)
    w_p = slot_w[:, 0].reshape(-1)
    w_m = slot_w[:, 1:].reshape(-1)

    def dispatch(place, weights):
        rows = place.shape[0]
        x = mm(place, tokens).astype(BF).reshape(devices_n, rows // devices_n, width)
        dy = (mm(place, cotangent) * weights[:, None]).astype(BF)
        dy = dy.reshape(devices_n, rows // devices_n, width)
        return exchange(x).reshape(rows, width), exchange(dy).reshape(rows, width)

    x_p, dy_p = dispatch(place_p, w_p)
    x_m, dy_m = dispatch(place_m, w_m)

    plain_w = [one(w, plain_slot) for w in (gate_weight, up_weight, down_weight)]
    overlap = jnp.arange(half, dtype=jnp.int32) < (2 * half - neurons)
    cover_m = jnp.where(i_am_src & overlap, 0.0, 1.0).astype(F32)
    cover_m = jnp.broadcast_to(cover_m[None, :], (8, half))
    cover_p = jnp.ones((8, neurons), F32)
    h_p, dg_p, du_p = hidden_block(x_p, dy_p, *plain_w, cover_p, 0)
    h_m, dg_m, du_m = hidden_block(x_m, dy_m, merged[0], merged[1], merged[2], cover_m, 1)

    def grads(x, dy, h, dg, du):
        return [mm_tn(x, dg).astype(BF), mm_tn(x, du).astype(BF), mm_tn(dy, h).astype(BF)]

    grads_m = jnp.concatenate(grads(x_m, dy_m, h_m, dg_m, du_m), axis=0)
    far = relay(grads_m[:, half - tail :])
    y_m = mm_nt(h_m, merged[2]).astype(BF)
    back_m = exchange(y_m.reshape(devices_n, -1, width)).reshape(-1, width)
    y_p = mm_nt(h_p, plain_w[2]).astype(BF)
    back_p = exchange(y_p.reshape(devices_n, -1, width)).reshape(-1, width)
    grads_p = grads(x_p, dy_p, h_p, dg_p, du_p)

    def combine(place, weights, back):
        hi = weights.astype(BF)
        lo = (weights - hi.astype(F32)).astype(BF)
        return mm_tn(place * hi[:, None], back) + mm_tn(place * lo[:, None], back)

    mixed = (combine(place_p, w_p, back_p) + combine(place_m, w_m, back_m)).astype(BF)

    outs = []
    for index, plain in enumerate(grads_p):
        rows = slice(index * width, (index + 1) * width)
        full = jnp.concatenate([grads_m[rows], far[rows]], axis=1)
        full = jnp.where(i_am_src, jnp.zeros_like(full), full)
        first_is_merge = merge_slot == 0
        outs.append(
            jnp.stack([jnp.where(first_is_merge, full, plain), jnp.where(first_is_merge, plain, full)])
        )
    return (mixed, *outs)


def solution(mesh):
    placed = (
        P("expert", "hidden"),
        P("expert", "hidden"),
        P("expert", "hidden", None),
        P("expert", "hidden", None),
        P("expert", "hidden", None),
        P("expert", None),
        P("expert", None),
        P(),
        P(),
        P(),
    )
    return jax.shard_map(
        shards,
        mesh=mesh,
        in_specs=placed,
        out_specs=(
            P("expert", "hidden"),
            P("expert", "hidden", None),
            P("expert", "hidden", None),
            P("expert", "hidden", None),
        ),
        check_vma=False,
    )
```

```python
import jax
import jax.numpy as jnp
from jax import lax
from jax.experimental import pallas as pl
from jax.experimental.pallas import tpu as pltpu
from jax.sharding import PartitionSpec as P

BF = jnp.bfloat16
F32 = jnp.float32
MESH = pl.DeviceIdType.MESH
N_HID = 4


def silu_parts(values):
    sigma = jax.nn.sigmoid(values)
    return (values * sigma, sigma * (1.0 + values * (1.0 - sigma)))


def mm(a, b):
    return jnp.dot(a, b, preferred_element_type=F32)


def mm_nt(a, b):
    return lax.dot_general(a, b, (((1,), (1,)), ((), ())), preferred_element_type=F32)


def mm_tn(a, b):
    return lax.dot_general(a, b, (((0,), (0,)), ((), ())), preferred_element_type=F32)


def add_to(ref, other):
    ref[...] = (ref[...].astype(F32) + other[...].astype(F32)).astype(BF)


class Ring:
    def __init__(self, part, in_a, in_b, in_l, in_r, full, sends, recvs):
        self.part, self.in_a, self.in_b, self.in_l, self.in_r = part, in_a, in_b, in_l, in_r
        self.full, self.sends, self.recvs = full, sends, recvs
        self.me = lax.axis_index("hidden")
        self.right = lax.rem(self.me + 1, N_HID)
        self.left = lax.rem(self.me + 3, N_HID)
        self.across = lax.rem(self.me + 2, N_HID)
        self.chunk = part.shape[2]
        self.lo = pl.ds(0, self.chunk // 2)
        self.hi = pl.ds(self.chunk // 2, self.chunk // 2)
        self.copies = {}

    def send(self, src, dst, kind, q, peer):
        copy = pltpu.make_async_remote_copy(
            src_ref=src,
            dst_ref=dst,
            send_sem=self.sends.at[kind, q],
            recv_sem=self.recvs.at[kind, q],
            device_id={"hidden": peer},
            device_id_type=MESH,
        )
        copy.start()
        self.copies[kind, q] = copy

    def start(self, q, product):
        part = self.part
        part[q, self.across] = product(self.across).astype(BF)
        self.send(part.at[q, self.across, self.lo], self.in_a.at[q], 0, q, self.right)
        self.send(part.at[q, self.across, self.hi], self.in_b.at[q], 1, q, self.left)

    def rest(self, q, product):
        for index in (self.right, self.left, self.me):
            self.part[q, index] = product(index).astype(BF)

    def second(self, q):
        part = self.part
        self.copies[0, q].wait_recv()
        add_to(part.at[q, self.right, self.lo], self.in_a.at[q])
        self.send(part.at[q, self.right], self.in_l.at[q], 2, q, self.right)
        self.copies[1, q].wait_recv()
        add_to(part.at[q, self.left, self.hi], self.in_b.at[q])
        self.send(part.at[q, self.left], self.in_r.at[q], 3, q, self.left)

    def acts(self, cover):
        for q in range(3):
            self.copies[2, q].wait_recv()
            self.copies[3, q].wait_recv()
        step = 32

        @pl.loop(0, self.chunk // step)
        def _(tile):
            rows = pl.ds(pl.multiple_of(tile * step, step), step)

            def total(q):
                own = self.part[q, self.me, rows].astype(F32)
                return own + self.in_l[q, rows].astype(F32) + self.in_r[q, rows].astype(F32)

            g, u, dh = total(0), total(1), total(2)
            active, slope = silu_parts(g)
            values = (active * u, dh * u * slope, dh * active)
            for q in range(3):
                value = values[q] if cover is None else values[q] * cover
                self.full[q, self.me, rows] = value.astype(BF)

    def publish(self, q):
        mine = self.full.at[q, self.me]
        self.send(mine, mine, 4, q, self.right)
        self.send(mine, mine, 5, q, self.left)

    def forward(self, q):
        self.copies[4, q].wait_recv()
        half = self.full.at[q, self.left, self.lo]
        self.send(half, half, 6, q, self.right)
        self.copies[5, q].wait_recv()
        half = self.full.at[q, self.right, self.hi]
        self.send(half, half, 7, q, self.left)

    def arrived(self, q):
        self.copies[6, q].wait_recv()
        self.copies[7, q].wait_recv()

    def sent(self, kinds):
        for kind in kinds:
            for q in range(3):
                self.copies[kind, q].wait_send()


def mega_kernel(
    table,
    tokens,
    cot,
    place,
    place_hi,
    place_lo,
    gate,
    up,
    down,
    send_ids,
    keep_ids,
    cover_ref,
    mixed,
    out_p,
    out_m,
    out_far,
    hot,
    sx_p,
    sx_m,
    rx_p,
    rx_m,
    w_send,
    w_mid0,
    w_mid1,
    w_mid2,
    w_got,
    w_keep,
    part_p,
    a_p,
    b_p,
    l_p,
    r_p,
    full_p,
    part_m,
    a_m,
    b_m,
    l_m,
    r_m,
    full_m,
    g_mid0,
    g_mid1,
    g_mid2,
    g_far,
    back_p,
    back_m,
    ring_ps,
    ring_pr,
    ring_ms,
    ring_mr,
    a2a_s,
    a2a_r,
    out_s,
):
    n = lax.axis_size("expert")
    me = lax.axis_index("expert")
    slot = table[n]
    weights = (gate, up, down)
    w_mid = (w_mid0, w_mid1, w_mid2)
    g_mid = (g_mid0, g_mid1, g_mid2)
    width = tokens.shape[1]
    neurons = gate.shape[2]
    half = w_keep.shape[2]
    far = g_far.shape[2]
    skip = half - far
    piece = width // n
    rows_p, rows_m = sx_p.shape[1], sx_m.shape[1]
    dp, dm = rows_p // n, rows_m // n
    y_z = n // 2

    def peer(step):
        flip = lax.rem(step, 2)
        shift = lax.div(step, 2)
        core = lax.rem(me, 2)
        node = lax.div(me, 2)
        side = 4 if y_z == 16 else y_z
        hi, lo = lax.div(node, side), lax.rem(node, side)
        dhi, dlo = lax.div(shift, side), lax.rem(shift, side)
        hi = lax.rem(hi + dhi, y_z // side)
        lo = lax.rem(lo + dlo, side)
        return (hi * side + lo) * 2 + lax.rem(core + flip, 2)

    ring_p = Ring(part_p, a_p, b_p, l_p, r_p, full_p, ring_ps, ring_pr)
    ring_m = Ring(part_m, a_m, b_m, l_m, r_m, full_m, ring_ms, ring_mr)

    barrier = pltpu.get_barrier_semaphore()
    for other in (ring_p.left, ring_p.right):
        pl.semaphore_signal(barrier, inc=1, device_id={"hidden": other}, device_id_type=MESH)

    @pl.loop(1, n)
    def _(step):
        pl.semaphore_signal(barrier, inc=1, device_id={"expert": peer(step)}, device_id_type=MESH)

    def scatter(sem, src_of, dst_of):
        @pl.loop(1, n)
        def _(step):
            other = peer(step)
            pltpu.make_async_remote_copy(
                src_ref=src_of(other),
                dst_ref=dst_of(me),
                send_sem=a2a_s.at[sem],
                recv_sem=a2a_r.at[sem],
                device_id={"expert": other},
                device_id_type=MESH,
            ).start()

    def landed(sem, ref):
        pltpu.make_async_copy(ref, ref, a2a_r.at[sem]).wait()

    def left_here(sem, ref):
        pltpu.make_async_copy(ref, ref, a2a_s.at[sem]).wait()

    def block(index, size):
        return pl.ds(pl.multiple_of(index * size, size), size)

    def build(base, rows, out):
        @pl.loop(0, rows // 128)
        def _(tile):
            src = pl.ds(pl.multiple_of(base + tile * 128, 128), 128)
            dst = block(tile, 128)
            out[0, dst] = mm(place[src, :], tokens[...]).astype(BF)
            out[1, dst] = (mm(place_hi[src, :], cot[...]) + mm(place_lo[src, :], cot[...])).astype(BF)

    build(0, rows_p, sx_p)
    pl.semaphore_wait(barrier, n + 1)

    scatter(0, lambda d: sx_p.at[:, block(d, dp)], lambda m: rx_p.at[:, block(m, dp)])
    rx_p[:, block(me, dp)] = sx_p[:, block(me, dp)]

    def ordered(ids, q, out):
        @pl.loop(0, width // 128)
        def _(tile):
            rows = block(tile, 128)
            out[q, rows] = mm(weights[q][slot, rows, :], hot[...]).astype(BF)

    def fill_hot(ids):
        @pl.loop(0, neurons // 128)
        def _(tile):
            rows = lax.broadcasted_iota(jnp.int32, (128, half), 0) + tile * 128
            hot[block(tile, 128)] = jnp.where(rows == ids[0:1, :], 1.0, 0.0).astype(BF)

    fill_hot(send_ids)
    for q in range(3):
        ordered(send_ids, q, w_send)
        scatter(1 + q, lambda d: w_send.at[q, block(d, piece)], lambda m: w_mid[q].at[m])
        w_mid[q][me] = w_send[q, block(me, piece)]

    build(rows_p, rows_m, sx_m)
    scatter(7, lambda d: sx_m.at[0, block(d, dm)], lambda m: rx_m.at[0, block(m, dm)])
    rx_m[0, block(me, dm)] = sx_m[0, block(me, dm)]
    rx_m[1, block(me, dm)] = sx_m[1, block(me, dm)]
    fill_hot(keep_ids)
    for q in range(3):
        ordered(keep_ids, q, w_keep)

    landed(0, rx_p.at[:, pl.ds(0, (n - 1) * dp)])
    lefts = (0, 0, 1)

    def product_p(q):
        def product(index):
            return mm(rx_p[lefts[q], block(index, ring_p.chunk), :], weights[q][1 - slot])

        return product

    def product_m(q):
        def product(index):
            return mm(rx_m[lefts[q], block(index, ring_m.chunk), :], w_keep[q])

        return product

    for q in range(3):
        ring_p.start(q, product_p(q))
    for q in range(3):
        ring_p.rest(q, product_p(q))

    def hop(q, mid, cols, first, then, dst_of):
        landed(first, mid[q].at[pl.ds(0, n - 1)])
        left_here(first, mid[q].at[pl.ds(0, n - 1)])

        @pl.loop(0, n)
        def _(other):
            w_send[q, block(other, piece), cols] = mid[q][table[other]]

        scatter(then, lambda d: w_send.at[q, block(d, piece), cols], dst_of(q))

    every = pl.ds(0, half)
    got_of = lambda q: lambda m: w_got.at[q, block(m, piece)]
    ring_p.second(0)
    hop(0, w_mid, every, 1, 4, got_of)
    w_got[0, block(me, piece)] = w_send[0, block(me, piece)]
    scatter(8, lambda d: sx_m.at[1, block(d, dm)], lambda m: rx_m.at[1, block(m, dm)])
    ring_p.second(1)
    hop(1, w_mid, every, 2, 5, got_of)
    w_got[1, block(me, piece)] = w_send[1, block(me, piece)]
    ring_p.second(2)
    hop(2, w_mid, every, 3, 6, got_of)
    w_got[2, block(me, piece)] = w_send[2, block(me, piece)]

    def blend(q):
        landed(4 + q, w_got.at[q, pl.ds(0, (n - 1) * piece)])

        @pl.loop(0, width // 128)
        def _(tile):
            rows = block(tile, 128)
            both = w_keep[q, rows].astype(F32) + w_got[q, rows].astype(F32)
            w_keep[q, rows] = (0.5 * both).astype(BF)

    landed(7, rx_m.at[0, pl.ds(0, (n - 1) * dm)])
    blend(0)
    ring_m.start(0, product_m(0))
    ring_m.rest(0, product_m(0))
    ring_p.acts(None)
    ring_p.publish(0)
    ring_m.second(0)
    blend(1)
    ring_m.start(1, product_m(1))
    ring_m.rest(1, product_m(1))
    ring_p.forward(0)
    landed(8, rx_m.at[1, pl.ds(0, (n - 1) * dm)])
    blend(2)
    ring_m.start(2, product_m(2))
    ring_m.rest(2, product_m(2))
    ring_m.second(1)
    ring_m.second(2)

    left_here(0, sx_p.at[:, pl.ds(0, (n - 1) * dp)])
    ring_p.arrived(0)
    for index in range(N_HID):
        rows = pl.ds(index * ring_p.chunk, ring_p.chunk)
        sx_p[0, rows] = mm_nt(full_p[0, index], weights[2][1 - slot]).astype(BF)
    scatter(9, lambda d: sx_p.at[0, block(d, dp)], lambda m: back_p.at[block(m, dp)])
    back_p[block(me, dp)] = sx_p[0, block(me, dp)]

    def gradient(left, full, rows, q, store):
        @pl.loop(0, width // 128)
        def _(tile):
            cols = block(tile, 128)
            right = full[q].reshape(rows, full.shape[3])
            store(tile, mm_tn(left[:, cols], right).astype(BF))

    ring_p.sent((0, 1, 2, 3))

    def store_p(q):
        def store(tile, value):
            part_p[q, tile] = value

        return store

    def store_m(q):
        def store(tile, value):
            part_m[q, lax.div(tile, 2), block(lax.rem(tile, 2), 128)] = value

        return store

    def grads_p(q, target):
        gradient(rx_p.at[1 if q == 0 else 0], full_p, rows_p, q, store_p(target))
        pltpu.make_async_copy(part_p.at[target], out_p.at[target], out_s.at[target]).start()

    cover = cover_ref[0:1, :]
    ring_m.acts(cover)
    ring_m.publish(0)
    ring_m.publish(1)
    grads_p(0, 2)
    ring_m.forward(0)
    ring_m.publish(2)
    ring_m.forward(1)
    ring_p.publish(1)
    ring_p.publish(2)

    def grads_m(q, target):
        gradient(rx_m.at[1 if q == 0 else 0], full_m, rows_m, q, store_m(target))
        pltpu.make_async_copy(part_m.at[target, pl.ds(0, 2)], out_m.at[target], out_s.at[3 + target]).start()

        def src(d):
            rows = block(lax.rem(d, n // 2), piece)
            return part_m.at[target, lax.div(d, n // 2), rows, pl.ds(skip, far)]

        scatter(11 + target, src, lambda m: g_mid[target].at[m])
        rows = block(lax.rem(me, n // 2), piece)
        g_mid[target][me] = part_m[target, lax.div(me, n // 2), rows, pl.ds(skip, far)]

    ring_m.arrived(0)
    ring_m.sent((0, 1, 2, 3))
    grads_m(0, 2)
    ring_m.forward(2)
    left_here(7, sx_m.at[0, pl.ds(0, (n - 1) * dm)])
    for index in range(N_HID):
        rows = pl.ds(index * ring_m.chunk, ring_m.chunk)
        sx_m[0, rows] = mm_nt(full_m[0, index], w_keep[2]).astype(BF)
    scatter(10, lambda d: sx_m.at[0, block(d, dm)], lambda m: back_m.at[block(m, dm)])
    back_m[block(me, dm)] = sx_m[0, block(me, dm)]
    ring_m.arrived(1)
    grads_m(1, 0)
    ring_p.forward(1)
    ring_m.arrived(2)
    grads_m(2, 1)
    ring_p.forward(2)

    for q in range(3):
        left_here(4 + q, w_mid[q].at[pl.ds(0, n - 1)])
    some = pl.ds(0, far)
    far_of = lambda q: lambda m: g_far.at[q, block(m, piece)]
    for q in (2, 0, 1):
        hop(q, g_mid, some, 11 + q, 14 + q, far_of)
        g_far[q, block(me, piece)] = w_send[q, block(me, piece), some]

    ring_p.arrived(1)
    grads_p(1, 0)
    ring_p.arrived(2)
    grads_p(2, 1)

    landed(9, back_p.at[pl.ds(0, (n - 1) * dp)])
    landed(10, back_m.at[pl.ds(0, (n - 1) * dm)])
    span_p, span_m = pl.ds(0, rows_p), pl.ds(rows_p, rows_m)
    total = mm_tn(place_hi[span_p, :], back_p[...]) + mm_tn(place_lo[span_p, :], back_p[...])
    total += mm_tn(place_hi[span_m, :], back_m[...]) + mm_tn(place_lo[span_m, :], back_m[...])
    mixed[...] = total.astype(BF)

    for q in (2, 0, 1):
        landed(14 + q, g_far.at[q, pl.ds(0, (n - 1) * piece)])
        pltpu.make_async_copy(g_far.at[q], out_far.at[q], out_s.at[6 + q]).start()

    left_here(8, sx_m.at[1, pl.ds(0, (n - 1) * dm)])
    left_here(9, sx_p.at[0, pl.ds(0, (n - 1) * dp)])
    left_here(10, sx_m.at[0, pl.ds(0, (n - 1) * dm)])
    for q in range(3):
        left_here(14 + q, g_far.at[q, pl.ds(0, (n - 1) * piece)])
        pltpu.make_async_copy(part_p.at[q], out_p.at[q], out_s.at[q]).wait()
        pltpu.make_async_copy(part_m.at[q, pl.ds(0, 2)], out_m.at[q], out_s.at[3 + q]).wait()
        pltpu.make_async_copy(g_far.at[q], out_far.at[q], out_s.at[6 + q]).wait()
    for ring in (ring_p, ring_m):
        ring.sent((4, 5, 6, 7))


def mega(table, tokens, cot, place, place_hi, place_lo, gate, up, down, send_ids, keep_ids, cover, n, depth):
    width, neurons = gate.shape[1], gate.shape[2]
    half = send_ids.shape[1]
    far = neurons - half
    rows_p, rows_m = n * depth, 2 * n * depth
    piece = width // n
    cp, cm = rows_p // N_HID, rows_m // N_HID
    vmem = pl.BlockSpec(memory_space=pltpu.VMEM)
    smem = pl.BlockSpec(memory_space=pltpu.SMEM)
    hbm = pl.BlockSpec(memory_space=pl.ANY)

    def ring(chunk, cols):
        return [
            pltpu.VMEM((3, N_HID, chunk, cols), BF),
            pltpu.VMEM((3, chunk // 2, cols), BF),
            pltpu.VMEM((3, chunk // 2, cols), BF),
            pltpu.VMEM((3, chunk, cols), BF),
            pltpu.VMEM((3, chunk, cols), BF),
            pltpu.VMEM((3, N_HID, chunk, cols), BF),
        ]

    return pl.pallas_call(
        mega_kernel,
        out_shape=(
            jax.ShapeDtypeStruct(tokens.shape, BF),
            jax.ShapeDtypeStruct((3, width // 128, 128, neurons), BF),
            jax.ShapeDtypeStruct((3, 2, width // 2, half), BF),
            jax.ShapeDtypeStruct((3, width, far), BF),
        ),
        in_specs=[smem] + [vmem] * 11,
        out_specs=(vmem, hbm, hbm, hbm),
        scratch_shapes=[
            pltpu.VMEM((neurons, half), BF),
            pltpu.VMEM((2, rows_p, width), BF),
            pltpu.VMEM((2, rows_m, width), BF),
            pltpu.VMEM((2, rows_p, width), BF),
            pltpu.VMEM((2, rows_m, width), BF),
            pltpu.VMEM((3, width, half), BF),
            *[pltpu.VMEM((n, piece, half), BF)] * 3,
            pltpu.VMEM((3, width, half), BF),
            pltpu.VMEM((3, width, half), BF),
            *ring(cp, neurons),
            *ring(cm, half),
            *[pltpu.VMEM((n, piece, far), BF)] * 3,
            pltpu.VMEM((3, width, far), BF),
            pltpu.VMEM((rows_p, width), BF),
            pltpu.VMEM((rows_m, width), BF),
            pltpu.SemaphoreType.DMA((8, 3)),
            pltpu.SemaphoreType.DMA((8, 3)),
            pltpu.SemaphoreType.DMA((8, 3)),
            pltpu.SemaphoreType.DMA((8, 3)),
            pltpu.SemaphoreType.DMA((17,)),
            pltpu.SemaphoreType.DMA((17,)),
            pltpu.SemaphoreType.DMA((9,)),
        ],
        compiler_params=pltpu.CompilerParams(
            collective_id=0, has_side_effects=True, vmem_limit_bytes=67_043_328
        ),
    )(table, tokens, cot, place, place_hi, place_lo, gate, up, down, send_ids, keep_ids, cover)


def shards(
    tokens,
    cotangent,
    gate_weight,
    up_weight,
    down_weight,
    routing,
    route_weight,
    merge_source,
    merge_target,
    neuron_perm,
):
    devices_n = lax.axis_size("expert")
    me = lax.axis_index("expert")
    exp_local, width, neurons = gate_weight.shape
    experts = exp_local * devices_n
    half = -(-neurons // 256) * 128
    tail = neurons - half
    tok_local, top_count = routing.shape
    depth = max(2, tok_local * top_count * 4 // (3 * experts))
    device_ids = jnp.arange(devices_n, dtype=jnp.int32)

    src_hit = (merge_source[:, None] // exp_local) == device_ids[None, :]
    tgt_hit = (merge_target[:, None] // exp_local) == device_ids[None, :]
    any_hit = src_hit | tgt_hit

    def pick(hit, values):
        return jnp.sum(jnp.where(hit, values[:, None], 0), axis=0)

    source_of = pick(any_hit, merge_source)
    target_of = pick(any_hit, merge_target)
    is_src = jnp.any(src_hit, axis=0)
    own_merge = jnp.where(is_src, source_of, target_of)
    partner_dev = jnp.where(is_src, target_of, source_of) // exp_local
    plain_of = device_ids * exp_local * 2 + (exp_local - 1) - own_merge
    i_am_src = jnp.any((merge_source // exp_local) == me)
    merge_slot = jnp.sum(jnp.where(device_ids == me, own_merge, 0)) - me * exp_local
    table = jnp.concatenate([partner_dev, jnp.full((8,), merge_slot, jnp.int32)])

    mine = ((merge_source // exp_local) == me) | ((merge_target // exp_local) == me)
    perm = jnp.sum(jnp.where(mine[:, None], neuron_perm, 0), axis=0)
    ids = jnp.arange(neurons, dtype=jnp.int32)
    send_ids = jnp.where(i_am_src, perm[:half], ids[tail:])
    keep_ids = jnp.where(i_am_src, perm[tail:], ids[:half])
    send_ids = jnp.broadcast_to(send_ids[None, :], (8, half))
    keep_ids = jnp.broadcast_to(keep_ids[None, :], (8, half))
    overlap = jnp.arange(half, dtype=jnp.int32) < (half - tail)
    cover = jnp.broadcast_to(jnp.where(i_am_src & overlap, 0.0, 1.0).astype(F32)[None, :], (8, half))

    def placing(slot_expert):
        hit = routing.T[None, :, :] == slot_expert[:, None, None]
        chosen = jnp.any(hit, axis=1)
        chosen_w = jnp.sum(jnp.where(hit, route_weight.T[None, :, :], 0.0), axis=1)
        tok_ids = jnp.arange(tok_local, dtype=jnp.int32)
        before = (tok_ids[:, None] < tok_ids[None, :]).astype(BF)
        rank = mm(chosen.astype(BF), before).astype(jnp.int32)
        rank = jnp.where(chosen, rank, -1)
        place = rank[:, None, :] == jnp.arange(depth, dtype=jnp.int32)[None, :, None]
        hi = chosen_w.astype(BF)
        lo = (chosen_w - hi.astype(F32)).astype(BF)
        zero = jnp.zeros((), BF)

        def filled(value):
            return jnp.where(place, value, zero).reshape(-1, tok_local)

        return filled(jnp.ones((), BF)), filled(hi[:, None, :]), filled(lo[:, None, :])

    slot_expert = jnp.concatenate([plain_of, jnp.stack([target_of, source_of], axis=1).reshape(-1)])
    place, place_hi, place_lo = placing(slot_expert)

    mixed, grads_p, grads_m, far = mega(
        table,
        tokens,
        cotangent,
        place,
        place_hi,
        place_lo,
        gate_weight,
        up_weight,
        down_weight,
        send_ids,
        keep_ids,
        cover,
        devices_n,
        depth,
    )
    grads_p = grads_p.reshape(3, width, neurons)
    grads_m = grads_m.reshape(3, width, half)

    outs = []
    for q in range(3):
        full = jnp.concatenate([grads_m[q], far[q]], axis=1)
        full = jnp.where(i_am_src, jnp.zeros_like(full), full)
        plain = grads_p[q]
        first_is_merge = merge_slot == 0
        outs.append(
            jnp.stack([jnp.where(first_is_merge, full, plain), jnp.where(first_is_merge, plain, full)])
        )
    return (mixed, *outs)


def solution(mesh):
    placed = (
        P("expert", "hidden"),
        P("expert", "hidden"),
        P("expert", "hidden", None),
        P("expert", "hidden", None),
        P("expert", "hidden", None),
        P("expert", None),
        P("expert", None),
        P(),
        P(),
        P(),
    )
    return jax.shard_map(
        shards,
        mesh=mesh,
        in_specs=placed,
        out_specs=(
            P("expert", "hidden"),
            P("expert", "hidden", None),
            P("expert", "hidden", None),
            P("expert", "hidden", None),
        ),
        check_vma=False,
    )
```

```python
import jax
import jax.numpy as jnp
from jax import lax
from jax.experimental import pallas as pl
from jax.experimental.pallas import tpu as pltpu
from jax.sharding import PartitionSpec as P

BF = jnp.bfloat16
F32 = jnp.float32
MESH = pl.DeviceIdType.MESH
N_HID = 4


def silu_parts(values):
    sigma = jax.nn.sigmoid(values)
    return (values * sigma, sigma * (1.0 + values * (1.0 - sigma)))


def mm(a, b):
    return jnp.dot(a, b, preferred_element_type=F32)


def mm_nt(a, b):
    return lax.dot_general(a, b, (((1,), (1,)), ((), ())), preferred_element_type=F32)


def mm_tn(a, b):
    return lax.dot_general(a, b, (((0,), (0,)), ((), ())), preferred_element_type=F32)


def add_to(ref, other):
    ref[...] = (ref[...].astype(F32) + other[...].astype(F32)).astype(BF)


class Ring:
    def __init__(self, part, in_a, in_b, in_l, in_r, full, sends, recvs):
        self.part, self.in_a, self.in_b, self.in_l, self.in_r = part, in_a, in_b, in_l, in_r
        self.full, self.sends, self.recvs = full, sends, recvs
        self.me = lax.axis_index("hidden")
        self.right = lax.rem(self.me + 1, N_HID)
        self.left = lax.rem(self.me + 3, N_HID)
        self.across = lax.rem(self.me + 2, N_HID)
        self.chunk = part.shape[2]
        self.lo = pl.ds(0, self.chunk // 2)
        self.hi = pl.ds(self.chunk // 2, self.chunk // 2)
        self.copies = {}

    def send(self, src, dst, kind, q, peer):
        copy = pltpu.make_async_remote_copy(
            src_ref=src,
            dst_ref=dst,
            send_sem=self.sends.at[kind, q],
            recv_sem=self.recvs.at[kind, q],
            device_id={"hidden": peer},
            device_id_type=MESH,
        )
        copy.start()
        self.copies[kind, q] = copy

    def start(self, q, product):
        part = self.part
        part[q, self.across] = product(self.across).astype(BF)
        self.send(part.at[q, self.across, self.lo], self.in_a.at[q], 0, q, self.right)
        self.send(part.at[q, self.across, self.hi], self.in_b.at[q], 1, q, self.left)

    def rest(self, q, product):
        for index in (self.right, self.left, self.me):
            self.part[q, index] = product(index).astype(BF)

    def second(self, q):
        part = self.part
        self.copies[0, q].wait_recv()
        add_to(part.at[q, self.right, self.lo], self.in_a.at[q])
        self.send(part.at[q, self.right], self.in_l.at[q], 2, q, self.right)
        self.copies[1, q].wait_recv()
        add_to(part.at[q, self.left, self.hi], self.in_b.at[q])
        self.send(part.at[q, self.left], self.in_r.at[q], 3, q, self.left)

    def acts(self, cover):
        for q in range(3):
            self.copies[2, q].wait_recv()
            self.copies[3, q].wait_recv()
        step = 32

        @pl.loop(0, self.chunk // step)
        def _(tile):
            rows = pl.ds(pl.multiple_of(tile * step, step), step)

            def total(q):
                own = self.part[q, self.me, rows].astype(F32)
                return own + self.in_l[q, rows].astype(F32) + self.in_r[q, rows].astype(F32)

            g, u, dh = total(0), total(1), total(2)
            active, slope = silu_parts(g)
            values = (active * u, dh * u * slope, dh * active)
            for q in range(3):
                value = values[q] if cover is None else values[q] * cover
                self.full[q, self.me, rows] = value.astype(BF)

    def publish(self, q):
        mine = self.full.at[q, self.me]
        self.send(mine, mine, 4, q, self.right)
        self.send(mine, mine, 5, q, self.left)

    def forward(self, q):
        self.copies[4, q].wait_recv()
        half = self.full.at[q, self.left, self.lo]
        self.send(half, half, 6, q, self.right)
        self.copies[5, q].wait_recv()
        half = self.full.at[q, self.right, self.hi]
        self.send(half, half, 7, q, self.left)

    def arrived(self, q):
        self.copies[6, q].wait_recv()
        self.copies[7, q].wait_recv()

    def sent(self, kinds):
        for kind in kinds:
            for q in range(3):
                self.copies[kind, q].wait_send()


def mega_kernel(
    sources,
    targets,
    perm_ref,
    routing,
    route_w,
    tokens,
    cot,
    gate_hbm,
    up_hbm,
    down_hbm,
    mixed,
    out_p,
    out_m,
    table,
    gate,
    up,
    down,
    place,
    place_hi,
    place_lo,
    hot,
    sx_p,
    sx_m,
    rx_p,
    rx_m,
    w_send,
    w_mid_a,
    w_mid_b,
    w_got,
    w_keep,
    part_p,
    a_p,
    b_p,
    l_p,
    r_p,
    full_p,
    part_a,
    a_a,
    b_a,
    l_a,
    r_a,
    full_a,
    part_b,
    a_b,
    b_b,
    l_b,
    r_b,
    full_b,
    g_mid_a,
    g_mid_b,
    g_far_a,
    g_far_b,
    back_p,
    back_m,
    ring_sems,
    a2a_s,
    a2a_r,
    in_s,
    out_s,
):
    n = lax.axis_size("expert")
    me = lax.axis_index("expert")
    weights = (gate, up, down)
    width = tokens.shape[1]
    tok_n, top = routing.shape
    neurons = gate.shape[2]
    half = w_keep.shape[2]
    tail = neurons - half
    cols_a, cols_b = full_a.shape[3], full_b.shape[3]
    far_a = g_far_a.shape[3]
    skip = cols_a - far_a
    piece = width // n
    rows_p, rows_m = sx_p.shape[1], sx_m.shape[1]
    dp, dm = rows_p // n, rows_m // n
    log_dp = dp.bit_length() - 1
    span_a, span_b = pl.ds(0, cols_a), pl.ds(cols_a, cols_b)

    def block(index, size):
        return pl.ds(pl.multiple_of(index * size, size), size)

    loads = []
    for q, ref in enumerate((gate_hbm, up_hbm, down_hbm)):
        loads.append(pltpu.make_async_copy(ref, weights[q], in_s.at[q]))
        loads[q].start()

    def peer(step):
        nodes = n // 2
        side = 4 if nodes == 16 else nodes
        core, node = lax.rem(me, 2), lax.div(me, 2)
        flip, shift = lax.rem(step, 2), lax.div(step, 2)
        hi = lax.rem(lax.div(node, side) + lax.div(shift, side), nodes // side)
        lo = lax.rem(lax.rem(node, side) + lax.rem(shift, side), side)
        return (hi * side + lo) * 2 + lax.rem(core + flip, 2)

    ring_p = Ring(part_p, a_p, b_p, l_p, r_p, full_p, ring_sems.at[0], ring_sems.at[1])
    ring_a = Ring(part_a, a_a, b_a, l_a, r_a, full_a, ring_sems.at[2], ring_sems.at[3])
    ring_b = Ring(part_b, a_b, b_b, l_b, r_b, full_b, ring_sems.at[4], ring_sems.at[5])

    barrier = pltpu.get_barrier_semaphore()
    for other in (ring_p.left, ring_p.right):
        pl.semaphore_signal(barrier, inc=1, device_id={"hidden": other}, device_id_type=MESH)

    @pl.loop(1, n)
    def _(step):
        pl.semaphore_signal(barrier, inc=1, device_id={"expert": peer(step)}, device_id_type=MESH)

    pairs = sources.shape[0]
    wide = rows_p
    log_wide = log_dp

    def make_place(tile):
        lane = lax.broadcasted_iota(jnp.int32, (8, wide), 1)
        if tile == 0:
            device = lax.shift_right_logical(lane, log_dp)
        else:
            lane = lane + (tile - 1) * wide
            device = lax.shift_right_logical(lane, log_dp + 1)
        source = jnp.zeros((8, wide), jnp.int32)
        target = jnp.zeros((8, wide), jnp.int32)
        own = jnp.zeros((8, wide), jnp.int32)
        for m in range(pairs):
            s, t = sources[m], targets[m]
            at_s, at_t = device == lax.shift_right_logical(s, 1), device == lax.shift_right_logical(t, 1)
            source = jnp.where(at_s | at_t, s, source)
            target = jnp.where(at_s | at_t, t, target)
            own = jnp.where(at_s, s, jnp.where(at_t, t, own))
        if tile == 0:
            expert = device * 4 + 1 - own
        else:
            is_target = (lax.shift_right_logical(lane, log_dp) & 1) == 0
            expert = jnp.where(is_target, target, source)
        expert = expert[0:1, :]
        chosen = jnp.zeros((tok_n, wide), F32)
        weight = jnp.zeros((tok_n, wide), F32)
        for k in range(top):
            hit = routing[:, k : k + 1] == expert
            chosen = jnp.where(hit, 1.0, chosen)
            weight = jnp.where(hit, route_w[:, k : k + 1], weight)
        row = lax.broadcasted_iota(jnp.int32, (tok_n, tok_n), 0)
        col = lax.broadcasted_iota(jnp.int32, (tok_n, tok_n), 1)
        before = jnp.where(col < row, 1.0, 0.0).astype(BF)
        rank = mm(before, chosen.astype(BF))
        slot_of = (lane[0:1, :] & (dp - 1)).astype(F32)
        here = (rank == slot_of) & (chosen > 0.5)
        hi = weight.astype(BF).astype(F32)
        span = pl.ds(tile * wide, wide)
        place[:, span] = jnp.where(here, 1.0, 0.0).astype(BF)
        place_hi[:, span] = jnp.where(here, hi, 0.0).astype(BF)
        place_lo[:, span] = jnp.where(here, weight - hi, 0.0).astype(BF)

    def build_x(base, rows, out):
        @pl.loop(0, rows // 128)
        def _(tile):
            src = pl.ds(pl.multiple_of(base + tile * 128, 128), 128)
            out[0, block(tile, 128)] = mm_tn(place[:, src], tokens[...]).astype(BF)

    def build_dy(base, rows, out):
        @pl.loop(0, rows // 128)
        def _(tile):
            src = pl.ds(pl.multiple_of(base + tile * 128, 128), 128)
            value = mm_tn(place_hi[:, src], cot[...]) + mm_tn(place_lo[:, src], cot[...])
            out[1, block(tile, 128)] = value.astype(BF)

    def scatter(sem, src_of, dst_of):
        @pl.loop(1, n)
        def _(step):
            other = peer(step)
            pltpu.make_async_remote_copy(
                src_ref=src_of(other),
                dst_ref=dst_of(me),
                send_sem=a2a_s.at[sem],
                recv_sem=a2a_r.at[sem],
                device_id={"expert": other},
                device_id_type=MESH,
            ).start()

    def landed(sem, ref):
        pltpu.make_async_copy(ref, ref, a2a_r.at[sem]).wait()

    def left_here(sem, ref):
        pltpu.make_async_copy(ref, ref, a2a_s.at[sem]).wait()

    all_p, all_m, peers = pl.ds(0, (n - 1) * dp), pl.ds(0, (n - 1) * dm), pl.ds(0, n - 1)

    def dispatch(sem, which, size, src, dst):
        scatter(sem, lambda d: src.at[which, block(d, size)], lambda m: dst.at[which, block(m, size)])
        dst[which, block(me, size)] = src[which, block(me, size)]

    make_place(0)
    build_x(0, rows_p, sx_p)
    pl.semaphore_wait(barrier, n + 1)
    dispatch(0, 0, dp, sx_p, rx_p)
    build_dy(0, rows_p, sx_p)
    dispatch(1, 1, dp, sx_p, rx_p)

    slot, is_src = jnp.int32(0), jnp.int32(0)
    for m in range(pairs):
        s, t = sources[m], targets[m]
        at_s, at_t = lax.shift_right_logical(s, 1) == me, lax.shift_right_logical(t, 1) == me
        slot = jnp.where(at_s, s & 1, jnp.where(at_t, t & 1, slot))
        is_src = jnp.where(at_s, 1, is_src)

    def fill_table(device, carry):
        partner = jnp.int32(0)
        for m in range(pairs):
            s, t = lax.shift_right_logical(sources[m], 1), lax.shift_right_logical(targets[m], 1)
            partner = jnp.where(s == device, t, jnp.where(t == device, s, partner))
        table[device] = partner
        return carry

    perm = jnp.zeros((8, neurons), jnp.int32)
    for m in range(pairs):
        s, t = lax.shift_right_logical(sources[m], 1), lax.shift_right_logical(targets[m], 1)
        mine = jnp.where((s == me) | (t == me), 1, 0)
        perm = perm + perm_ref[m : m + 1, :] * mine
    perm = perm[0:1, :]
    lane = lax.broadcasted_iota(jnp.int32, (1, half), 1)
    send_ids = jnp.where(is_src > 0, perm[:, :half], lane + tail)
    keep_ids = jnp.where(is_src > 0, perm[:, tail:], lane)

    def ordered(ids, span, out):
        @pl.loop(0, neurons // 128)
        def _(tile):
            units = ids[:, span.start : span.start + span.size]
            rows = lax.broadcasted_iota(jnp.int32, (128, span.size), 0) + tile * 128
            hot[block(tile, 128), span] = jnp.where(rows == units, 1.0, 0.0).astype(BF)

        for q in range(3):

            @pl.loop(0, width // 128)
            def _(tile):
                rows = block(tile, 128)
                out[q, rows, span] = mm(weights[q][slot, rows, :], hot[:, span]).astype(BF)

    def first_hop(sem, span, mid):
        scatter(sem, lambda d: w_send.at[:, block(d, piece), span], lambda m: mid.at[m])
        mid[me] = w_send[:, block(me, piece), span]

    def second_hop(first, then, mid, span, dst_of):
        landed(first, mid.at[peers])
        left_here(first, mid.at[peers])

        @pl.loop(0, n)
        def _(other):
            w_send[:, block(other, piece), span] = mid[table[other]]

        scatter(then, lambda d: w_send.at[:, block(d, piece), span], dst_of)

    for load in loads:
        load.wait()
    ordered(send_ids, span_a, w_send)
    first_hop(2, span_a, w_mid_a)
    make_place(1)
    make_place(2)
    build_x(rows_p, rows_m, sx_m)
    dispatch(6, 0, dm, sx_m, rx_m)

    lefts = (0, 0, 1)

    def product_p(q):
        def product(index):
            return mm(rx_p[lefts[q], block(index, ring_p.chunk), :], weights[q][1 - slot])

        return product

    def product_m(ring, q, span):
        def product(index):
            return mm(rx_m[lefts[q], block(index, ring.chunk), :], w_keep[q, :, span])

        return product

    landed(0, rx_p.at[0, all_p])
    ring_p.start(0, product_p(0))
    ring_p.start(1, product_p(1))
    landed(1, rx_p.at[1, all_p])
    ring_p.start(2, product_p(2))
    ring_p.rest(0, product_p(0))
    ring_p.second(0)
    ring_p.rest(1, product_p(1))
    ring_p.second(1)
    ring_p.rest(2, product_p(2))
    ring_p.second(2)
    lax.fori_loop(0, n, fill_table, 0)
    build_dy(rows_p, rows_m, sx_m)
    ordered(send_ids, span_b, w_send)

    got_of = lambda span: lambda m: w_got.at[:, block(m, piece), span]
    second_hop(2, 4, w_mid_a, span_a, got_of(span_a))
    w_got[:, block(me, piece), span_a] = w_send[:, block(me, piece), span_a]
    dispatch(7, 1, dm, sx_m, rx_m)
    first_hop(3, span_b, w_mid_b)
    ordered(keep_ids, span_a, w_keep)
    ordered(keep_ids, span_b, w_keep)

    def blend(sem, span):
        landed(sem, w_got.at[:, pl.ds(0, (n - 1) * piece), span])
        for q in range(3):

            @pl.loop(0, width // 128)
            def _(tile):
                rows = block(tile, 128)
                both = w_keep[q, rows, span].astype(F32) + w_got[q, rows, span].astype(F32)
                w_keep[q, rows, span] = (0.5 * both).astype(BF)

    ring_p.acts(None)
    ring_p.publish(0)
    landed(6, rx_m.at[0, all_m])
    blend(4, span_a)
    for q in range(2):
        ring_a.start(q, product_m(ring_a, q, span_a))
    for q in range(2):
        ring_a.rest(q, product_m(ring_a, q, span_a))
    ring_a.second(0)
    ring_a.second(1)
    ring_p.forward(0)
    landed(7, rx_m.at[1, all_m])
    ring_a.start(2, product_m(ring_a, 2, span_a))
    ring_a.rest(2, product_m(ring_a, 2, span_a))
    ring_a.second(2)
    second_hop(3, 5, w_mid_b, span_b, got_of(span_b))
    w_got[:, block(me, piece), span_b] = w_send[:, block(me, piece), span_b]

    ring_p.arrived(0)
    left_here(0, sx_p.at[0, all_p])
    for index in range(N_HID):
        rows = pl.ds(index * ring_p.chunk, ring_p.chunk)
        sx_p[0, rows] = mm_nt(full_p[0, index], weights[2][1 - slot]).astype(BF)
    scatter(8, lambda d: sx_p.at[0, block(d, dp)], lambda m: back_p.at[block(m, dp)])
    back_p[block(me, dp)] = sx_p[0, block(me, dp)]

    unit = lax.broadcasted_iota(jnp.int32, (1, cols_a), 1)
    cover = jnp.where((unit < skip) & (is_src > 0), 0.0, 1.0).astype(F32)
    ring_a.acts(cover)
    ring_a.publish(0)
    ring_a.publish(1)
    ring_a.publish(2)

    blend(5, span_b)
    for q in range(3):
        ring_b.start(q, product_m(ring_b, q, span_b))
    ring_a.forward(0)
    for q in range(3):
        ring_b.rest(q, product_m(ring_b, q, span_b))
    ring_a.forward(1)
    ring_b.second(0)
    ring_b.second(1)
    ring_a.forward(2)
    ring_b.second(2)

    def gradient(left, full, rows, q, store):
        @pl.loop(0, width // 128)
        def _(tile):
            right = full[q].reshape(rows, full.shape[3])
            store(tile, mm_tn(left[:, block(tile, 128)], right).astype(BF))

    def grads_p(q, target):
        def store(tile, value):
            part_p[target, tile] = value

        gradient(rx_p.at[1 if q == 0 else 0], full_p, rows_p, q, store)
        pltpu.make_async_copy(part_p.at[target], out_p.at[target], out_s.at[target]).start()

    halves = pl.ds(0, 2)
    jobs = []

    def put(src, dst):
        copy = pltpu.make_async_copy(src, dst, out_s.at[3 + len(jobs)])
        copy.start()
        jobs.append(copy)

    def grads_m(ring, q, target, base):
        def store(tile, value):
            ring.part[target, lax.div(tile, 2), block(lax.rem(tile, 2), 128)] = value

        gradient(rx_m.at[1 if q == 0 else 0], ring.full, rows_m, q, store)
        put(ring.part.at[target, halves], out_m.at[target, :, :, pl.ds(base, ring.part.shape[3])])

    def grad_hop(ring, sem, base, size, mid):
        def src(d):
            rows = block(lax.rem(d, n // 2), piece)
            return ring.part.at[:, lax.div(d, n // 2), rows, pl.ds(base, size)]

        scatter(sem, src, lambda m: mid.at[m])
        rows = block(lax.rem(me, n // 2), piece)
        mid[me] = ring.part[:, lax.div(me, n // 2), rows, pl.ds(base, size)]

    def far_of(far):
        return lambda m: far.at[:, lax.div(m, n // 2), block(lax.rem(m, n // 2), piece), :]

    def far_own(far, span):
        rows = block(lax.rem(me, n // 2), piece)
        far[:, lax.div(me, n // 2), rows, :] = w_send[:, block(me, piece), span]

    ring_a.sent((0, 1, 2, 3))
    for q, target in ((0, 2), (1, 0), (2, 1)):
        ring_a.arrived(q)
        if q == 1:
            ring_b.acts(None)
            ring_b.publish(0)
            ring_b.publish(1)
            ring_b.publish(2)
        grads_m(ring_a, q, target, 0)
    grad_hop(ring_a, 10, skip, far_a, g_mid_a)
    ring_b.forward(0)
    ring_b.forward(1)
    ring_b.forward(2)
    ring_p.publish(1)
    ring_p.publish(2)
    ring_p.sent((0, 1, 2, 3))
    ring_b.sent((0, 1, 2, 3))
    left_here(6, sx_m.at[0, all_m])
    ring_b.arrived(0)
    grads_m(ring_b, 0, 2, cols_a)
    left_here(4, w_mid_a.at[peers])
    spare_a, spare_b = pl.ds(0, far_a), span_b
    ring_b.arrived(1)
    grads_m(ring_b, 1, 0, cols_a)
    ring_b.arrived(2)
    grads_m(ring_b, 2, 1, cols_a)
    grad_hop(ring_b, 11, 0, cols_b, g_mid_b)
    second_hop(10, 12, g_mid_a, spare_a, far_of(g_far_a))
    far_own(g_far_a, spare_a)
    ring_p.forward(1)

    for index in range(N_HID):
        rows = pl.ds(index * ring_a.chunk, ring_a.chunk)
        value = mm_nt(full_a[0, index], w_keep[2, :, span_a]) + mm_nt(full_b[0, index], w_keep[2, :, span_b])
        sx_m[0, rows] = value.astype(BF)
    scatter(9, lambda d: sx_m.at[0, block(d, dm)], lambda m: back_m.at[block(m, dm)])
    back_m[block(me, dm)] = sx_m[0, block(me, dm)]
    ring_p.forward(2)
    left_here(5, w_mid_b.at[peers])
    second_hop(11, 13, g_mid_b, spare_b, far_of(g_far_b))
    far_own(g_far_b, spare_b)
    grads_p(0, 2)
    ring_p.arrived(1)
    grads_p(1, 0)
    ring_p.arrived(2)
    grads_p(2, 1)

    far_rows = pl.ds(0, n // 2 - 1)
    all_far = g_mid_a.at[peers]
    landed(12, all_far)
    for q in range(3):
        put(g_far_a.at[q], out_m.at[q, :, :, pl.ds(half, far_a)])

    landed(8, back_p.at[all_p])
    landed(9, back_m.at[all_m])
    span_p, span_m = pl.ds(0, rows_p), pl.ds(rows_p, rows_m)
    total = mm(place_hi[:, span_p], back_p[...]) + mm(place_lo[:, span_p], back_p[...])
    total += mm(place_hi[:, span_m], back_m[...]) + mm(place_lo[:, span_m], back_m[...])
    mixed[...] = total.astype(BF)

    landed(13, g_mid_b.at[peers])
    for q in range(3):
        put(g_far_b.at[q], out_m.at[q, :, :, pl.ds(half + far_a, cols_b)])

    left_here(1, sx_p.at[1, all_p])
    left_here(7, sx_m.at[1, all_m])
    left_here(8, sx_p.at[0, all_p])
    left_here(9, sx_m.at[0, all_m])
    left_here(12, g_mid_a.at[peers])
    left_here(13, g_mid_b.at[peers])
    for ring in (ring_p, ring_a, ring_b):
        ring.sent((4, 5, 6, 7))
    for q in range(3):
        pltpu.make_async_copy(part_p.at[q], out_p.at[q], out_s.at[q]).wait()
    for job in jobs:
        job.wait()


def mega(sources, targets, perm, routing, route_w, tokens, cot, gate, up, down, n, depth):
    width, neurons = gate.shape[1], gate.shape[2]
    half = -(-neurons // 256) * 128
    far = neurons - half
    cols_a = (half * 2 // 3) // 128 * 128
    cols_b = half - cols_a
    far_a = far - cols_b
    rows_p, rows_m = n * depth, 2 * n * depth
    piece = width // n
    cp, cm = rows_p // N_HID, rows_m // N_HID
    vmem = pl.BlockSpec(memory_space=pltpu.VMEM)
    smem = pl.BlockSpec(memory_space=pltpu.SMEM)
    hbm = pl.BlockSpec(memory_space=pl.ANY)

    def ring(chunk, cols):
        return [
            pltpu.VMEM((3, N_HID, chunk, cols), BF),
            pltpu.VMEM((3, chunk // 2, cols), BF),
            pltpu.VMEM((3, chunk // 2, cols), BF),
            pltpu.VMEM((3, chunk, cols), BF),
            pltpu.VMEM((3, chunk, cols), BF),
            pltpu.VMEM((3, N_HID, chunk, cols), BF),
        ]

    return pl.pallas_call(
        mega_kernel,
        out_shape=(
            jax.ShapeDtypeStruct(tokens.shape, BF),
            jax.ShapeDtypeStruct((3, width // 128, 128, neurons), BF),
            jax.ShapeDtypeStruct((3, 2, width // 2, neurons), BF),
        ),
        in_specs=[smem] * 2 + [vmem] * 5 + [hbm] * 3,
        out_specs=(vmem, hbm, hbm),
        scratch_shapes=[
            pltpu.SMEM((n,), jnp.int32),
            *[pltpu.VMEM(gate.shape, BF)] * 3,
            *[pltpu.VMEM((tokens.shape[0], rows_p + rows_m), BF)] * 3,
            pltpu.VMEM((neurons, half), BF),
            pltpu.VMEM((2, rows_p, width), BF),
            pltpu.VMEM((2, rows_m, width), BF),
            pltpu.VMEM((2, rows_p, width), BF),
            pltpu.VMEM((2, rows_m, width), BF),
            pltpu.VMEM((3, width, half), BF),
            pltpu.VMEM((n, 3, piece, cols_a), BF),
            pltpu.VMEM((n, 3, piece, cols_b), BF),
            pltpu.VMEM((3, width, half), BF),
            pltpu.VMEM((3, width, half), BF),
            *ring(cp, neurons),
            *ring(cm, cols_a),
            *ring(cm, cols_b),
            pltpu.VMEM((n, 3, piece, far_a), BF),
            pltpu.VMEM((n, 3, piece, cols_b), BF),
            pltpu.VMEM((3, 2, width // 2, far_a), BF),
            pltpu.VMEM((3, 2, width // 2, cols_b), BF),
            pltpu.VMEM((rows_p, width), BF),
            pltpu.VMEM((rows_m, width), BF),
            pltpu.SemaphoreType.DMA((6, 8, 3)),
            pltpu.SemaphoreType.DMA((14,)),
            pltpu.SemaphoreType.DMA((14,)),
            pltpu.SemaphoreType.DMA((3,)),
            pltpu.SemaphoreType.DMA((15,)),
        ],
        compiler_params=pltpu.CompilerParams(
            collective_id=0, has_side_effects=True, vmem_limit_bytes=67_043_328
        ),
    )(sources, targets, perm, routing, route_w, tokens, cot, gate, up, down)


def shards(
    tokens,
    cotangent,
    gate_weight,
    up_weight,
    down_weight,
    routing,
    route_weight,
    merge_source,
    merge_target,
    neuron_perm,
):
    devices_n = lax.axis_size("expert")
    me = lax.axis_index("expert")
    exp_local, width, neurons = gate_weight.shape
    tok_local, top_count = routing.shape
    depth = max(2, tok_local * top_count * 4 // (3 * exp_local * devices_n))
    mixed, grads_p, grads_m = mega(
        merge_source,
        merge_target,
        neuron_perm,
        routing,
        route_weight,
        tokens,
        cotangent,
        gate_weight,
        up_weight,
        down_weight,
        devices_n,
        depth,
    )
    grads_p = grads_p.reshape(3, width, neurons)
    grads_m = grads_m.reshape(3, width, neurons)

    of_source = jnp.where(merge_source // exp_local == me, 2 + merge_source % exp_local, 0)
    of_target = jnp.where(merge_target // exp_local == me, merge_target % exp_local, 0)
    role = jnp.sum(of_source + of_target)
    place = jnp.arange(exp_local, dtype=jnp.int32)[:, None, None]
    is_merge = place == role % 2

    def final(q):
        merged = jnp.where(role >= 2, jnp.zeros((), BF), grads_m[q][None])
        return jnp.where(is_merge, merged, grads_p[q][None])

    return (mixed, final(0), final(1), final(2))


def solution(mesh):
    placed = (
        P("expert", "hidden"),
        P("expert", "hidden"),
        P("expert", "hidden", None),
        P("expert", "hidden", None),
        P("expert", "hidden", None),
        P("expert", None),
        P("expert", None),
        P(),
        P(),
        P(),
    )
    return jax.shard_map(
        shards,
        mesh=mesh,
        in_specs=placed,
        out_specs=(
            P("expert", "hidden"),
            P("expert", "hidden", None),
            P("expert", "hidden", None),
            P("expert", "hidden", None),
        ),
        check_vma=False,
    )
```

```python
import jax
import jax.numpy as jnp
from jax import lax
from jax.experimental import pallas as pl
from jax.experimental.pallas import tpu as pltpu
from jax.sharding import PartitionSpec as P

BF = jnp.bfloat16
F32 = jnp.float32
MESH = pl.DeviceIdType.MESH
N_HID = 4
BLOCKS = 3


def silu_parts(values):
    sigma = jax.nn.sigmoid(values)
    return (values * sigma, sigma * (1.0 + values * (1.0 - sigma)))


def mm(a, b):
    return jnp.dot(a, b, preferred_element_type=F32)


def mm_nt(a, b):
    return lax.dot_general(a, b, (((1,), (1,)), ((), ())), preferred_element_type=F32)


def mm_tn(a, b):
    return lax.dot_general(a, b, (((0,), (0,)), ((), ())), preferred_element_type=F32)


def add_to(ref, other):
    ref[...] = (ref[...].astype(F32) + other[...].astype(F32)).astype(BF)


class Ring:
    def __init__(self, part, in_a, in_b, in_l, in_r, full, sends, recvs):
        self.part, self.in_a, self.in_b, self.in_l, self.in_r = part, in_a, in_b, in_l, in_r
        self.full, self.sends, self.recvs = full, sends, recvs
        self.me = lax.axis_index("hidden")
        self.right = lax.rem(self.me + 1, N_HID)
        self.left = lax.rem(self.me + 3, N_HID)
        self.across = lax.rem(self.me + 2, N_HID)
        self.chunk = part.shape[2]
        self.lo = pl.ds(0, self.chunk // 2)
        self.hi = pl.ds(self.chunk // 2, self.chunk // 2)
        self.copies = {}

    def send(self, src, dst, kind, q, peer):
        copy = pltpu.make_async_remote_copy(
            src_ref=src,
            dst_ref=dst,
            send_sem=self.sends.at[kind, q],
            recv_sem=self.recvs.at[kind, q],
            device_id={"hidden": peer},
            device_id_type=MESH,
        )
        copy.start()
        self.copies[kind, q] = copy

    def start(self, q, product):
        part = self.part
        part[q, self.across] = product(self.across).astype(BF)
        self.send(part.at[q, self.across, self.lo], self.in_a.at[q], 0, q, self.right)
        self.send(part.at[q, self.across, self.hi], self.in_b.at[q], 1, q, self.left)

    def rest(self, q, product):
        for index in (self.right, self.left, self.me):
            self.part[q, index] = product(index).astype(BF)

    def second(self, q):
        part = self.part
        self.copies[0, q].wait_recv()
        add_to(part.at[q, self.right, self.lo], self.in_a.at[q])
        self.send(part.at[q, self.right], self.in_l.at[q], 2, q, self.right)
        self.copies[1, q].wait_recv()
        add_to(part.at[q, self.left, self.hi], self.in_b.at[q])
        self.send(part.at[q, self.left], self.in_r.at[q], 3, q, self.left)

    def acts(self, cover):
        for q in range(3):
            self.copies[2, q].wait_recv()
            self.copies[3, q].wait_recv()
        step = 32

        @pl.loop(0, self.chunk // step)
        def _(tile):
            rows = pl.ds(pl.multiple_of(tile * step, step), step)

            def total(q):
                own = self.part[q, self.me, rows].astype(F32)
                return own + self.in_l[q, rows].astype(F32) + self.in_r[q, rows].astype(F32)

            g, u, dh = total(0), total(1), total(2)
            active, slope = silu_parts(g)
            values = (active * u, dh * u * slope, dh * active)
            for q in range(3):
                value = values[q] if cover is None else values[q] * cover
                self.full[q, self.me, rows] = value.astype(BF)

    def publish(self, q):
        mine = self.full.at[q, self.me]
        self.send(mine, mine, 4, q, self.right)
        self.send(mine, mine, 5, q, self.left)

    def forward(self, q):
        self.copies[4, q].wait_recv()
        half = self.full.at[q, self.left, self.lo]
        self.send(half, half, 6, q, self.right)
        self.copies[5, q].wait_recv()
        half = self.full.at[q, self.right, self.hi]
        self.send(half, half, 7, q, self.left)

    def arrived(self, q):
        self.copies[6, q].wait_recv()
        self.copies[7, q].wait_recv()

    def sent(self, kinds):
        for kind in kinds:
            for q in range(3):
                self.copies[kind, q].wait_send()


def mega_kernel(
    sources,
    targets,
    perm_ref,
    routing,
    route_w,
    tokens,
    cot,
    gate_hbm,
    up_hbm,
    down_hbm,
    mixed,
    role,
    out_p,
    out_m,
    *scratch,
):
    scratch = list(scratch)

    def take(count):
        got = scratch[:count]
        del scratch[:count]
        return got

    table, weights, columns, place, place_hi, place_lo, hot, sx_p, sx_m, rx_p, rx_m = take(11)
    w_send, w_got, w_keep, back_p, back_m = take(5)
    w_mid, g_mid, g_far = take(BLOCKS), take(BLOCKS), take(BLOCKS)
    scraps = [take(6) for _ in range(1 + BLOCKS)]
    ring_sems, a2a_s, a2a_r, in_s, out_s = take(5)
    n = lax.axis_size("expert")
    me = lax.axis_index("expert")
    width = tokens.shape[1]
    top, tok_n = routing.shape
    neurons = weights.shape[3]
    half = w_keep.shape[2]
    tail = neurons - half
    cols = half // BLOCKS
    skip = 2 * half - neurons
    piece = width // n
    rows_p, rows_m = sx_p.shape[1], sx_m.shape[1]
    dp, dm = rows_p // n, rows_m // n
    log_dp = dp.bit_length() - 1
    spans = [pl.ds(i * cols, cols) for i in range(BLOCKS)]
    cut = [skip] + [0] * (BLOCKS - 1)

    def block(index, size):
        return pl.ds(pl.multiple_of(index * size, size), size)

    loads = []
    for q, ref in enumerate((gate_hbm, up_hbm, down_hbm)):
        loads.append(pltpu.make_async_copy(ref, weights.at[q], in_s.at[q]))
        loads[q].start()

    def peer(step):
        nodes = n // 2
        side = 4 if nodes == 16 else nodes
        core, node = lax.rem(me, 2), lax.div(me, 2)
        flip, shift = lax.rem(step, 2), lax.div(step, 2)
        hi = lax.rem(lax.div(node, side) + lax.div(shift, side), nodes // side)
        lo = lax.rem(lax.rem(node, side) + lax.rem(shift, side), side)
        return (hi * side + lo) * 2 + lax.rem(core + flip, 2)

    rings = [Ring(*scraps[i], ring_sems.at[2 * i], ring_sems.at[2 * i + 1]) for i in range(1 + BLOCKS)]
    ring_p, blocks = rings[0], rings[1:]
    part_p, full_p = ring_p.part, ring_p.full

    barrier = pltpu.get_barrier_semaphore()
    for other in (ring_p.left, ring_p.right):
        pl.semaphore_signal(barrier, inc=1, device_id={"hidden": other}, device_id_type=MESH)

    @pl.loop(1, n)
    def _(step):
        pl.semaphore_signal(barrier, inc=1, device_id={"expert": peer(step)}, device_id_type=MESH)

    columns[...] = jnp.zeros_like(columns)
    columns[0, 0:top] = routing[...].astype(F32)
    columns[1, 0:top] = route_w[...]
    names, shares = jnp.transpose(columns[0]), jnp.transpose(columns[1])

    pairs = sources.shape[0]
    wide = rows_p
    log_wide = log_dp

    def make_place(tile):
        lane = lax.broadcasted_iota(jnp.int32, (8, wide), 1)
        if tile == 0:
            device = lax.shift_right_logical(lane, log_dp)
        else:
            lane = lane + (tile - 1) * wide
            device = lax.shift_right_logical(lane, log_dp + 1)
        source = jnp.zeros((8, wide), jnp.int32)
        target = jnp.zeros((8, wide), jnp.int32)
        own = jnp.zeros((8, wide), jnp.int32)
        for m in range(pairs):
            s, t = sources[m], targets[m]
            at_s, at_t = device == lax.shift_right_logical(s, 1), device == lax.shift_right_logical(t, 1)
            source = jnp.where(at_s | at_t, s, source)
            target = jnp.where(at_s | at_t, t, target)
            own = jnp.where(at_s, s, jnp.where(at_t, t, own))
        if tile == 0:
            expert = device * 4 + 1 - own
        else:
            is_target = (lax.shift_right_logical(lane, log_dp) & 1) == 0
            expert = jnp.where(is_target, target, source)
        expert = expert[0:1, :]
        chosen = jnp.zeros((tok_n, wide), F32)
        weight = jnp.zeros((tok_n, wide), F32)
        expert = expert.astype(F32)
        for k in range(top):
            hit = names[:, k : k + 1] == expert
            chosen = jnp.where(hit, 1.0, chosen)
            weight = jnp.where(hit, shares[:, k : k + 1], weight)
        row = lax.broadcasted_iota(jnp.int32, (tok_n, tok_n), 0)
        col = lax.broadcasted_iota(jnp.int32, (tok_n, tok_n), 1)
        before = jnp.where(col < row, 1.0, 0.0).astype(BF)
        rank = mm(before, chosen.astype(BF))
        slot_of = (lane[0:1, :] & (dp - 1)).astype(F32)
        here = (rank == slot_of) & (chosen > 0.5)
        hi = weight.astype(BF).astype(F32)
        span = pl.ds(tile * wide, wide)
        place[:, span] = jnp.where(here, 1.0, 0.0).astype(BF)
        place_hi[:, span] = jnp.where(here, hi, 0.0).astype(BF)
        place_lo[:, span] = jnp.where(here, weight - hi, 0.0).astype(BF)

    def build_x(base, rows, out):
        @pl.loop(0, rows // 128)
        def _(tile):
            src = pl.ds(pl.multiple_of(base + tile * 128, 128), 128)
            out[0, block(tile, 128)] = mm_tn(place[:, src], tokens[...]).astype(BF)

    def build_dy(base, rows, out):
        @pl.loop(0, rows // 128)
        def _(tile):
            src = pl.ds(pl.multiple_of(base + tile * 128, 128), 128)
            value = mm_tn(place_hi[:, src], cot[...]) + mm_tn(place_lo[:, src], cot[...])
            out[1, block(tile, 128)] = value.astype(BF)

    def scatter(sem, src_of, dst_of):
        @pl.loop(1, n)
        def _(step):
            other = peer(step)
            pltpu.make_async_remote_copy(
                src_ref=src_of(other),
                dst_ref=dst_of(me),
                send_sem=a2a_s.at[sem],
                recv_sem=a2a_r.at[sem],
                device_id={"expert": other},
                device_id_type=MESH,
            ).start()

    def landed(sem, ref):
        pltpu.make_async_copy(ref, ref, a2a_r.at[sem]).wait()

    def left_here(sem, ref):
        pltpu.make_async_copy(ref, ref, a2a_s.at[sem]).wait()

    all_p, all_m, peers = pl.ds(0, (n - 1) * dp), pl.ds(0, (n - 1) * dm), pl.ds(0, n - 1)

    def dispatch(sem, which, size, src, dst):
        scatter(sem, lambda d: src.at[which, block(d, size)], lambda m: dst.at[which, block(m, size)])
        dst[which, block(me, size)] = src[which, block(me, size)]

    make_place(0)
    build_x(0, rows_p, sx_p)
    pl.semaphore_wait(barrier, n + 1)
    dispatch(0, 0, dp, sx_p, rx_p)
    build_dy(0, rows_p, sx_p)
    dispatch(1, 1, dp, sx_p, rx_p)

    slot, is_src = jnp.int32(0), jnp.int32(0)
    for m in range(pairs):
        s, t = sources[m], targets[m]
        at_s, at_t = lax.shift_right_logical(s, 1) == me, lax.shift_right_logical(t, 1) == me
        slot = jnp.where(at_s, s & 1, jnp.where(at_t, t & 1, slot))
        is_src = jnp.where(at_s, 1, is_src)
    role[0] = is_src * 2 + slot

    def fill_table(device, carry):
        partner = jnp.int32(0)
        for m in range(pairs):
            s, t = lax.shift_right_logical(sources[m], 1), lax.shift_right_logical(targets[m], 1)
            partner = jnp.where(s == device, t, jnp.where(t == device, s, partner))
        table[device] = partner
        return carry

    perm = jnp.zeros((8, neurons), jnp.int32)
    for m in range(pairs):
        s, t = lax.shift_right_logical(sources[m], 1), lax.shift_right_logical(targets[m], 1)
        mine = jnp.where((s == me) | (t == me), 1, 0)
        perm = perm + perm_ref[m : m + 1, :] * mine
    perm = perm[0:1, :]
    lane = lax.broadcasted_iota(jnp.int32, (1, half), 1)
    send_ids = jnp.where(is_src > 0, perm[:, :half], lane + tail)
    keep_ids = jnp.where(is_src > 0, perm[:, tail:], lane)

    def ordered(ids, span, out):
        units = ids[:, span.start : span.start + span.size]

        @pl.loop(0, neurons // 128)
        def _(tile):
            rows = lax.broadcasted_iota(jnp.int32, (128, span.size), 0) + tile * 128
            hot[block(tile, 128)] = jnp.where(rows == units, 1.0, 0.0).astype(BF)

        @pl.loop(0, 3)
        def _(q):
            out[q, :, span] = mm(weights[q, slot], hot[...]).astype(BF)

    def first_hop(i):
        scatter(2 + i, lambda d: w_send.at[:, block(d, piece), spans[i]], lambda m: w_mid[i].at[m])
        w_mid[i][me] = w_send[:, block(me, piece), spans[i]]

    def second_hop(first, then, mid, span, dst_of):
        landed(first, mid.at[peers])
        left_here(first, mid.at[peers])

        @pl.loop(0, n)
        def _(other):
            w_send[:, block(other, piece), span] = mid[table[other]]

        scatter(then, lambda d: w_send.at[:, block(d, piece), span], dst_of)

    def weight_hop(i):
        second_hop(2 + i, 5 + i, w_mid[i], spans[i], lambda m: w_got.at[:, block(m, piece), spans[i]])
        w_got[:, block(me, piece), spans[i]] = w_send[:, block(me, piece), spans[i]]

    for load in loads:
        load.wait()
    ordered(send_ids, spans[0], w_send)
    first_hop(0)
    make_place(1)
    make_place(2)
    build_x(rows_p, rows_m, sx_m)
    dispatch(8, 0, dm, sx_m, rx_m)

    lefts = (0, 0, 1)

    def product_p(q):
        def product(index):
            return mm(rx_p[lefts[q], block(index, ring_p.chunk), :], weights[q, 1 - slot])

        return product

    def product_m(i, q):
        def product(index):
            return mm(rx_m[lefts[q], block(index, blocks[i].chunk), :], w_keep[q, :, spans[i]])

        return product

    landed(0, rx_p.at[0, all_p])
    ring_p.start(0, product_p(0))
    ring_p.start(1, product_p(1))
    build_dy(rows_p, rows_m, sx_m)
    dispatch(9, 1, dm, sx_m, rx_m)
    landed(1, rx_p.at[1, all_p])
    ring_p.start(2, product_p(2))
    ring_p.rest(0, product_p(0))
    ring_p.second(0)
    ring_p.rest(1, product_p(1))
    ring_p.second(1)
    lax.fori_loop(0, n, fill_table, 0)
    weight_hop(0)
    ring_p.rest(2, product_p(2))
    ring_p.second(2)
    for i in range(1, BLOCKS):
        ordered(send_ids, spans[i], w_send)
        first_hop(i)
    for i in range(BLOCKS):
        ordered(keep_ids, spans[i], w_keep)

    def blend(i):
        landed(5 + i, w_got.at[:, pl.ds(0, (n - 1) * piece), spans[i]])

        @pl.loop(0, 3 * (width // 128))
        def _(tile):
            q, rows = lax.div(tile, width // 128), block(lax.rem(tile, width // 128), 128)
            both = w_keep[q, rows, spans[i]].astype(F32) + w_got[q, rows, spans[i]].astype(F32)
            w_keep[q, rows, spans[i]] = (0.5 * both).astype(BF)

    def gradient(left, full, rows, q, store):
        tile_n = 256

        @pl.loop(0, width // tile_n)
        def _(tile):
            right = full[q].reshape(rows, full.shape[3])
            store(tile, mm_tn(left[:, block(tile, tile_n)], right).astype(BF))

    def grads_p(q, target):
        def store(tile, value):
            part_p[target, pl.ds(tile * 2, 2)] = value.reshape(2, 128, neurons)

        gradient(rx_p.at[1 if q == 0 else 0], full_p, rows_p, q, store)
        pltpu.make_async_copy(part_p.at[target], out_p.at[target], out_s.at[target]).start()

    halves = pl.ds(0, 2)
    jobs = []

    def put(src, dst):
        copy = pltpu.make_async_copy(src, dst, out_s.at[3 + len(jobs)])
        copy.start()
        jobs.append(copy)

    def grads_m(i, q, target):
        part = blocks[i].part

        def store(tile, value):
            part[target, tile] = value

        gradient(rx_m.at[1 if q == 0 else 0], blocks[i].full, rows_m, q, store)

    def grad_hop(i):
        part, mid = blocks[i].part, g_mid[i]
        size = pl.ds(cut[i], cols - cut[i])

        def src(d):
            return part.at[:, lax.div(d, n // 2), block(lax.rem(d, n // 2), piece), size]

        scatter(10 + i, src, lambda m: mid.at[m])
        mid[me] = part[:, lax.div(me, n // 2), block(lax.rem(me, n // 2), piece), size]
        for q in range(3):
            put(part.at[q, halves], out_m.at[q, :, :, spans[i]])

    def back_hop(i):
        far, size = g_far[i], pl.ds(i * cols, cols - cut[i])
        left_here(5 + i, w_mid[i].at[peers])

        def dst(m):
            return far.at[:, lax.div(m, n // 2), block(lax.rem(m, n // 2), piece), :]

        second_hop(10 + i, 13 + i, g_mid[i], size, dst)
        rows = block(lax.rem(me, n // 2), piece)
        far[:, lax.div(me, n // 2), rows, :] = w_send[:, block(me, piece), size]

    unit = lax.broadcasted_iota(jnp.int32, (1, cols), 1)
    cover = jnp.where((unit < skip) & (is_src > 0), 0.0, 1.0).astype(F32)

    def mix_outputs():
        landed(16, back_p.at[all_p])
        landed(17, back_m.at[all_m])
        span_p, span_m = pl.ds(0, rows_p), pl.ds(rows_p, rows_m)
        total = mm(place_hi[:, span_p], back_p[...]) + mm(place_lo[:, span_p], back_p[...])
        total += mm(place_hi[:, span_m], back_m[...]) + mm(place_lo[:, span_m], back_m[...])
        mixed[...] = total.astype(BF)

    def enter(i):
        blend(i)
        for q in range(3):
            blocks[i].start(q, product_m(i, q))

    def rest(i):
        for q in range(3):
            blocks[i].rest(q, product_m(i, q))

    def seconds(i):
        for q in range(3):
            blocks[i].second(q)

    def publish(i):
        blocks[i].acts(cover if i == 0 else None)
        for q in range(3):
            blocks[i].publish(q)

    def forwards(i):
        for q in range(3):
            blocks[i].forward(q)

    def leave(i):
        blocks[i].sent((0, 1, 2, 3))
        for q, target in ((0, 2), (1, 0), (2, 1)):
            blocks[i].arrived(q)
            grads_m(i, q, target)
        grad_hop(i)

    ring_p.acts(None)
    landed(8, rx_m.at[0, all_m])
    landed(9, rx_m.at[1, all_m])
    enter(0)
    ring_p.publish(0)
    rest(0)
    seconds(0)
    weight_hop(1)
    ring_p.forward(0)
    weight_hop(2)
    enter(1)
    rest(1)
    publish(0)
    seconds(1)
    forwards(0)

    ring_p.arrived(0)
    left_here(0, sx_p.at[0, all_p])
    for index in range(N_HID):
        rows = pl.ds(index * ring_p.chunk, ring_p.chunk)
        sx_p[0, rows] = mm_nt(full_p[0, index], weights[2, 1 - slot]).astype(BF)
    scatter(16, lambda d: sx_p.at[0, block(d, dp)], lambda m: back_p.at[block(m, dp)])
    back_p[block(me, dp)] = sx_p[0, block(me, dp)]

    enter(2)
    rest(2)
    publish(1)
    seconds(2)
    leave(0)
    forwards(1)
    back_hop(0)
    publish(2)
    leave(1)
    forwards(2)
    ring_p.publish(1)
    ring_p.publish(2)
    ring_p.sent((0, 1, 2, 3))
    left_here(8, sx_m.at[0, all_m])
    back_hop(1)
    leave(2)
    ring_p.forward(1)

    for index in range(N_HID):
        rows = pl.ds(index * blocks[0].chunk, blocks[0].chunk)
        value = mm_nt(blocks[0].full[0, index], w_keep[2, :, spans[0]])
        for i in range(1, BLOCKS):
            value += mm_nt(blocks[i].full[0, index], w_keep[2, :, spans[i]])
        sx_m[0, rows] = value.astype(BF)
    scatter(17, lambda d: sx_m.at[0, block(d, dm)], lambda m: back_m.at[block(m, dm)])
    back_m[block(me, dm)] = sx_m[0, block(me, dm)]
    ring_p.forward(2)
    back_hop(2)
    grads_p(0, 2)
    ring_p.arrived(1)
    grads_p(1, 0)
    ring_p.arrived(2)
    grads_p(2, 1)

    base = half
    for i in range(BLOCKS):
        if i == BLOCKS - 1:
            mix_outputs()
        landed(13 + i, g_mid[i].at[peers])
        for q in range(3):
            put(g_far[i].at[q], out_m.at[q, :, :, pl.ds(base, cols - cut[i])])
        base += cols - cut[i]

    left_here(1, sx_p.at[1, all_p])
    left_here(9, sx_m.at[1, all_m])
    left_here(16, sx_p.at[0, all_p])
    left_here(17, sx_m.at[0, all_m])
    for i in range(BLOCKS):
        left_here(13 + i, g_mid[i].at[peers])
    for ring in rings:
        ring.sent((4, 5, 6, 7))
    for q in range(3):
        pltpu.make_async_copy(part_p.at[q], out_p.at[q], out_s.at[q]).wait()
    for job in jobs:
        job.wait()


def mega(sources, targets, perm, routing, route_w, tokens, cot, gate, up, down, n, depth):
    width, neurons = gate.shape[1], gate.shape[2]
    half = -(-neurons // 256) * 128
    far = neurons - half
    cols = half // BLOCKS
    fars = [far - (BLOCKS - 1) * cols] + [cols] * (BLOCKS - 1)
    rows_p, rows_m = n * depth, 2 * n * depth
    piece = width // n
    cp, cm = rows_p // N_HID, rows_m // N_HID
    vmem = pl.BlockSpec(memory_space=pltpu.VMEM)
    smem = pl.BlockSpec(memory_space=pltpu.SMEM)
    hbm = pl.BlockSpec(memory_space=pl.ANY)

    def ring(chunk, cols):
        return [
            pltpu.VMEM((3, N_HID, chunk, cols), BF),
            pltpu.VMEM((3, chunk // 2, cols), BF),
            pltpu.VMEM((3, chunk // 2, cols), BF),
            pltpu.VMEM((3, chunk, cols), BF),
            pltpu.VMEM((3, chunk, cols), BF),
            pltpu.VMEM((3, N_HID, chunk, cols), BF),
        ]

    return pl.pallas_call(
        mega_kernel,
        out_shape=(
            jax.ShapeDtypeStruct(tokens.shape, BF),
            jax.ShapeDtypeStruct((1,), jnp.int32),
            jax.ShapeDtypeStruct((3, width // 128, 128, neurons), BF),
            jax.ShapeDtypeStruct((3, 2, width // 2, neurons), BF),
        ),
        in_specs=[smem] * 2 + [vmem] * 5 + [hbm] * 3,
        out_specs=(vmem, smem, hbm, hbm),
        scratch_shapes=[
            pltpu.SMEM((n,), jnp.int32),
            pltpu.VMEM((3, *gate.shape), BF),
            pltpu.VMEM((2, 8, tokens.shape[0]), F32),
            *[pltpu.VMEM((tokens.shape[0], rows_p + rows_m), BF)] * 3,
            pltpu.VMEM((neurons, cols), BF),
            pltpu.VMEM((2, rows_p, width), BF),
            pltpu.VMEM((2, rows_m, width), BF),
            pltpu.VMEM((2, rows_p, width), BF),
            pltpu.VMEM((2, rows_m, width), BF),
            *[pltpu.VMEM((3, width, half), BF)] * 3,
            pltpu.VMEM((rows_p, width), BF),
            pltpu.VMEM((rows_m, width), BF),
            *[pltpu.VMEM((n, 3, piece, cols), BF)] * BLOCKS,
            *[pltpu.VMEM((n, 3, piece, size), BF) for size in fars],
            *[pltpu.VMEM((3, 2, width // 2, size), BF) for size in fars],
            *ring(cp, neurons),
            *(ring(cm, cols) * BLOCKS),
            pltpu.SemaphoreType.DMA((2 + 2 * BLOCKS, 8, 3)),
            pltpu.SemaphoreType.DMA((18,)),
            pltpu.SemaphoreType.DMA((18,)),
            pltpu.SemaphoreType.DMA((3,)),
            pltpu.SemaphoreType.DMA((3 + 6 * BLOCKS,)),
        ],
        compiler_params=pltpu.CompilerParams(
            collective_id=0, has_side_effects=True, vmem_limit_bytes=67_043_328
        ),
    )(sources, targets, perm, routing, route_w, tokens, cot, gate, up, down)


def shards(
    tokens,
    cotangent,
    gate_weight,
    up_weight,
    down_weight,
    routing,
    route_weight,
    merge_source,
    merge_target,
    neuron_perm,
):
    devices_n = lax.axis_size("expert")
    exp_local, width, neurons = gate_weight.shape
    tok_local, top_count = routing.shape
    depth = max(2, tok_local * top_count * 4 // (3 * exp_local * devices_n))
    mixed, role, grads_p, grads_m = mega(
        merge_source,
        merge_target,
        neuron_perm,
        routing.T,
        route_weight.T,
        tokens,
        cotangent,
        gate_weight,
        up_weight,
        down_weight,
        devices_n,
        depth,
    )
    grads_p = grads_p.reshape(3, width, neurons)
    grads_m = grads_m.reshape(3, width, neurons)

    role = role[0]
    place = jnp.arange(exp_local, dtype=jnp.int32)[:, None, None]
    is_merge = place == role % 2

    def final(q):
        merged = jnp.where(role >= 2, jnp.zeros((), BF), grads_m[q][None])
        return jnp.where(is_merge, merged, grads_p[q][None])

    return (mixed, final(0), final(1), final(2))


def solution(mesh):
    placed = (
        P("expert", "hidden"),
        P("expert", "hidden"),
        P("expert", "hidden", None),
        P("expert", "hidden", None),
        P("expert", "hidden", None),
        P("expert", None),
        P("expert", None),
        P(),
        P(),
        P(),
    )
    return jax.shard_map(
        shards,
        mesh=mesh,
        in_specs=placed,
        out_specs=(
            P("expert", "hidden"),
            P("expert", "hidden", None),
            P("expert", "hidden", None),
            P("expert", "hidden", None),
        ),
        check_vma=False,
    )
```

```python
import jax
import jax.numpy as jnp
from jax import lax
from jax.experimental import pallas as pl
from jax.experimental.pallas import tpu as pltpu
from jax.sharding import PartitionSpec as P

BF = jnp.bfloat16
F32 = jnp.float32
MESH = pl.DeviceIdType.MESH
N_HID = 4
BLOCKS = 3


def silu_parts(values):
    sigma = jax.nn.sigmoid(values)
    return (values * sigma, sigma * (1.0 + values * (1.0 - sigma)))


def mm(a, b):
    return jnp.dot(a, b, preferred_element_type=F32)


def mm_nt(a, b):
    return lax.dot_general(a, b, (((1,), (1,)), ((), ())), preferred_element_type=F32)


def mm_tn(a, b):
    return lax.dot_general(a, b, (((0,), (0,)), ((), ())), preferred_element_type=F32)


def add_to(ref, other):
    ref[...] = (ref[...].astype(F32) + other[...].astype(F32)).astype(BF)


class Ring:
    def __init__(self, part, in_a, in_b, in_l, in_r, full, sends, recvs):
        self.part, self.in_a, self.in_b, self.in_l, self.in_r = part, in_a, in_b, in_l, in_r
        self.full, self.sends, self.recvs = full, sends, recvs
        self.me = lax.axis_index("hidden")
        self.right = lax.rem(self.me + 1, N_HID)
        self.left = lax.rem(self.me + 3, N_HID)
        self.across = lax.rem(self.me + 2, N_HID)
        self.chunk = part.shape[2]
        self.lo = pl.ds(0, self.chunk // 2)
        self.hi = pl.ds(self.chunk // 2, self.chunk // 2)
        self.copies = {}
        self.seen = set()

    def send(self, src, dst, kind, q, peer):
        copy = pltpu.make_async_remote_copy(
            src_ref=src,
            dst_ref=dst,
            send_sem=self.sends.at[kind, q],
            recv_sem=self.recvs.at[kind, q],
            device_id={"hidden": peer},
            device_id_type=MESH,
        )
        copy.start()
        self.copies[kind, q] = copy

    def start(self, q, product):
        part = self.part
        part[q, self.across] = product(self.across).astype(BF)
        self.send(part.at[q, self.across, self.lo], self.in_a.at[q], 0, q, self.right)
        self.send(part.at[q, self.across, self.hi], self.in_b.at[q], 1, q, self.left)

    def rest(self, q, product):
        for index in (self.right, self.left, self.me):
            self.part[q, index] = product(index).astype(BF)

    def second(self, q):
        part = self.part
        self.copies[0, q].wait_recv()
        add_to(part.at[q, self.right, self.lo], self.in_a.at[q])
        self.send(part.at[q, self.right], self.in_l.at[q], 2, q, self.right)
        self.copies[1, q].wait_recv()
        add_to(part.at[q, self.left, self.hi], self.in_b.at[q])
        self.send(part.at[q, self.left], self.in_r.at[q], 3, q, self.left)

    def acts(self, cover):
        for q in range(3):
            self.copies[2, q].wait_recv()
            self.copies[3, q].wait_recv()
        step = 32

        @pl.loop(0, self.chunk // step)
        def _(tile):
            rows = pl.ds(pl.multiple_of(tile * step, step), step)

            def total(q):
                own = self.part[q, self.me, rows].astype(F32)
                return own + self.in_l[q, rows].astype(F32) + self.in_r[q, rows].astype(F32)

            g, u, dh = total(0), total(1), total(2)
            active, slope = silu_parts(g)
            values = (active * u, dh * u * slope, dh * active)
            for q in range(3):
                value = values[q] if cover is None else values[q] * cover
                self.full[q, self.me, rows] = value.astype(BF)

    def publish(self, q):
        mine = self.full.at[q, self.me]
        self.send(mine, mine, 4, q, self.right)
        self.send(mine, mine, 5, q, self.left)

    def forward(self, q):
        self.copies[4, q].wait_recv()
        half = self.full.at[q, self.left, self.lo]
        self.send(half, half, 6, q, self.right)
        self.copies[5, q].wait_recv()
        half = self.full.at[q, self.right, self.hi]
        self.send(half, half, 7, q, self.left)

    def arrived(self, q):
        for kind in (6, 7):
            if (kind, q) not in self.seen:
                self.seen.add((kind, q))
                self.copies[kind, q].wait_recv()

    def sent(self, kinds):
        for kind in kinds:
            for q in range(3):
                self.copies[kind, q].wait_send()


def mega_kernel(
    sources,
    targets,
    perm_ref,
    routing,
    route_w,
    tokens,
    cot,
    gate_hbm,
    up_hbm,
    down_hbm,
    mixed,
    role,
    out_p,
    out_m,
    *scratch,
):
    scratch = list(scratch)

    def take(count):
        got = scratch[:count]
        del scratch[:count]
        return got

    table, weights, columns, place, place_hi, place_lo, hot, sx_p, sx_m, rx_p, rx_m = take(11)
    w_send, w_got, w_keep, back_p, back_m = take(5)
    w_mid, g_mid, g_far = take(BLOCKS), take(BLOCKS), take(BLOCKS)
    scraps = [take(6) for _ in range(1 + BLOCKS)]
    ring_sems, a2a_s, a2a_r, in_s, out_s = take(5)
    n = lax.axis_size("expert")
    me = lax.axis_index("expert")
    width = tokens.shape[1]
    top, tok_n = routing.shape
    neurons = weights.shape[3]
    half = w_keep.shape[2]
    tail = neurons - half
    cols = half // BLOCKS
    skip = 2 * half - neurons
    piece = width // n
    rows_p, rows_m = sx_p.shape[1], sx_m.shape[1]
    dp, dm = rows_p // n, rows_m // n
    log_dp = dp.bit_length() - 1
    spans = [pl.ds((i + 1) % BLOCKS * cols, cols) for i in range(BLOCKS)]
    cut = [0] * (BLOCKS - 1) + [skip]

    def block(index, size):
        return pl.ds(pl.multiple_of(index * size, size), size)

    loads = []
    for q, ref in enumerate((gate_hbm, up_hbm, down_hbm)):
        loads.append(pltpu.make_async_copy(ref, weights.at[q], in_s.at[q]))
        loads[q].start()

    def peer(step):
        nodes = n // 2
        side = 4 if nodes == 16 else nodes
        core, node = lax.rem(me, 2), lax.div(me, 2)
        flip, shift = lax.rem(step, 2), lax.div(step, 2)
        hi = lax.rem(lax.div(node, side) + lax.div(shift, side), nodes // side)
        lo = lax.rem(lax.rem(node, side) + lax.rem(shift, side), side)
        return (hi * side + lo) * 2 + lax.rem(core + flip, 2)

    rings = [Ring(*scraps[i], ring_sems.at[2 * i], ring_sems.at[2 * i + 1]) for i in range(1 + BLOCKS)]
    ring_p, blocks = rings[0], rings[1:]
    part_p, full_p = ring_p.part, ring_p.full

    barrier = pltpu.get_barrier_semaphore()
    for other in (ring_p.left, ring_p.right):
        pl.semaphore_signal(barrier, inc=1, device_id={"hidden": other}, device_id_type=MESH)

    @pl.loop(1, n)
    def _(step):
        pl.semaphore_signal(barrier, inc=1, device_id={"expert": peer(step)}, device_id_type=MESH)

    columns[...] = jnp.zeros_like(columns)
    columns[0, 0:top] = routing[...].astype(F32)
    columns[1, 0:top] = route_w[...]
    names, shares = jnp.transpose(columns[0]), jnp.transpose(columns[1])

    pairs = sources.shape[0]
    wide = rows_p
    log_wide = log_dp

    def make_place(tile):
        lane = lax.broadcasted_iota(jnp.int32, (8, wide), 1)
        if tile == 0:
            device = lax.shift_right_logical(lane, log_dp)
        else:
            lane = lane + (tile - 1) * wide
            device = lax.shift_right_logical(lane, log_dp + 1)
        source = jnp.zeros((8, wide), jnp.int32)
        target = jnp.zeros((8, wide), jnp.int32)
        own = jnp.zeros((8, wide), jnp.int32)
        for m in range(pairs):
            s, t = sources[m], targets[m]
            at_s, at_t = device == lax.shift_right_logical(s, 1), device == lax.shift_right_logical(t, 1)
            source = jnp.where(at_s | at_t, s, source)
            target = jnp.where(at_s | at_t, t, target)
            own = jnp.where(at_s, s, jnp.where(at_t, t, own))
        if tile == 0:
            expert = device * 4 + 1 - own
        else:
            is_target = (lax.shift_right_logical(lane, log_dp) & 1) == 0
            expert = jnp.where(is_target, target, source)
        expert = expert[0:1, :]
        chosen = jnp.zeros((tok_n, wide), F32)
        weight = jnp.zeros((tok_n, wide), F32)
        expert = expert.astype(F32)
        for k in range(top):
            hit = names[:, k : k + 1] == expert
            chosen = jnp.where(hit, 1.0, chosen)
            weight = jnp.where(hit, shares[:, k : k + 1], weight)
        row = lax.broadcasted_iota(jnp.int32, (tok_n, tok_n), 0)
        col = lax.broadcasted_iota(jnp.int32, (tok_n, tok_n), 1)
        before = jnp.where(col < row, 1.0, 0.0).astype(BF)
        rank = mm(before, chosen.astype(BF))
        slot_of = (lane[0:1, :] & (dp - 1)).astype(F32)
        here = (rank == slot_of) & (chosen > 0.5)
        hi = weight.astype(BF).astype(F32)
        span = pl.ds(tile * wide, wide)
        place[:, span] = jnp.where(here, 1.0, 0.0).astype(BF)
        place_hi[:, span] = jnp.where(here, hi, 0.0).astype(BF)
        place_lo[:, span] = jnp.where(here, weight - hi, 0.0).astype(BF)

    def build_x(base, rows, out):
        @pl.loop(0, rows // 128)
        def _(tile):
            src = pl.ds(pl.multiple_of(base + tile * 128, 128), 128)
            out[0, block(tile, 128)] = mm_tn(place[:, src], tokens[...]).astype(BF)

    def build_dy(base, rows, out):
        @pl.loop(0, rows // 128)
        def _(tile):
            src = pl.ds(pl.multiple_of(base + tile * 128, 128), 128)
            value = mm_tn(place_hi[:, src], cot[...]) + mm_tn(place_lo[:, src], cot[...])
            out[1, block(tile, 128)] = value.astype(BF)

    def scatter(sem, src_of, dst_of):
        @pl.loop(1, n)
        def _(step):
            other = peer(step)
            pltpu.make_async_remote_copy(
                src_ref=src_of(other),
                dst_ref=dst_of(me),
                send_sem=a2a_s.at[sem],
                recv_sem=a2a_r.at[sem],
                device_id={"expert": other},
                device_id_type=MESH,
            ).start()

    def landed(sem, ref):
        pltpu.make_async_copy(ref, ref, a2a_r.at[sem]).wait()

    def left_here(sem, ref):
        pltpu.make_async_copy(ref, ref, a2a_s.at[sem]).wait()

    all_p, all_m, peers = pl.ds(0, (n - 1) * dp), pl.ds(0, (n - 1) * dm), pl.ds(0, n - 1)

    def dispatch(sem, which, size, src, dst):
        scatter(sem, lambda d: src.at[which, block(d, size)], lambda m: dst.at[which, block(m, size)])
        dst[which, block(me, size)] = src[which, block(me, size)]

    make_place(0)
    build_x(0, rows_p, sx_p)
    pl.semaphore_wait(barrier, n + 1)
    dispatch(0, 0, dp, sx_p, rx_p)
    build_dy(0, rows_p, sx_p)
    dispatch(1, 1, dp, sx_p, rx_p)

    slot, is_src = jnp.int32(0), jnp.int32(0)
    for m in range(pairs):
        s, t = sources[m], targets[m]
        at_s, at_t = lax.shift_right_logical(s, 1) == me, lax.shift_right_logical(t, 1) == me
        slot = jnp.where(at_s, s & 1, jnp.where(at_t, t & 1, slot))
        is_src = jnp.where(at_s, 1, is_src)
    role[0] = is_src * 2 + slot

    def fill_table(device, carry):
        partner = jnp.int32(0)
        for m in range(pairs):
            s, t = lax.shift_right_logical(sources[m], 1), lax.shift_right_logical(targets[m], 1)
            partner = jnp.where(s == device, t, jnp.where(t == device, s, partner))
        table[device] = partner
        return carry

    perm = jnp.zeros((8, neurons), jnp.int32)
    for m in range(pairs):
        s, t = lax.shift_right_logical(sources[m], 1), lax.shift_right_logical(targets[m], 1)
        mine = jnp.where((s == me) | (t == me), 1, 0)
        perm = perm + perm_ref[m : m + 1, :] * mine
    perm = perm[0:1, :]
    lane = lax.broadcasted_iota(jnp.int32, (1, half), 1)
    send_ids = jnp.where(is_src > 0, perm[:, :half], lane + tail)
    keep_ids = jnp.where(is_src > 0, perm[:, tail:], lane)

    def ordered(ids, span, out):
        units = ids[:, span.start : span.start + span.size]

        @pl.loop(0, neurons // 128)
        def _(tile):
            rows = lax.broadcasted_iota(jnp.int32, (128, span.size), 0) + tile * 128
            hot[block(tile, 128)] = jnp.where(rows == units, 1.0, 0.0).astype(BF)

        @pl.loop(0, 3)
        def _(q):
            out[q, :, span] = mm(weights[q, slot], hot[...]).astype(BF)

    def first_hop(i):
        scatter(2 + i, lambda d: w_send.at[:, block(d, piece), spans[i]], lambda m: w_mid[i].at[m])
        w_mid[i][me] = w_send[:, block(me, piece), spans[i]]

    def second_hop(first, then, mid, span, dst_of):
        landed(first, mid.at[peers])
        left_here(first, mid.at[peers])

        @pl.loop(0, n)
        def _(other):
            w_send[:, block(other, piece), span] = mid[table[other]]

        scatter(then, lambda d: w_send.at[:, block(d, piece), span], dst_of)

    def weight_hop(i):
        second_hop(2 + i, 5 + i, w_mid[i], spans[i], lambda m: w_got.at[:, block(m, piece), spans[i]])
        w_got[:, block(me, piece), spans[i]] = w_send[:, block(me, piece), spans[i]]

    for load in loads:
        load.wait()
    ordered(send_ids, spans[0], w_send)
    first_hop(0)
    make_place(1)
    make_place(2)
    build_x(rows_p, rows_m, sx_m)
    dispatch(8, 0, dm, sx_m, rx_m)

    lefts = (0, 0, 1)

    def product_p(q):
        def product(index):
            return mm(rx_p[lefts[q], block(index, ring_p.chunk), :], weights[q, 1 - slot])

        return product

    def product_m(i, q):
        def product(index):
            return mm(rx_m[lefts[q], block(index, blocks[i].chunk), :], w_keep[q, :, spans[i]])

        return product

    landed(0, rx_p.at[0, all_p])
    ring_p.start(0, product_p(0))
    ring_p.start(1, product_p(1))
    build_dy(rows_p, rows_m, sx_m)
    landed(1, rx_p.at[1, all_p])
    ring_p.start(2, product_p(2))
    ring_p.rest(0, product_p(0))
    ring_p.second(0)
    ring_p.rest(1, product_p(1))
    ring_p.second(1)
    lax.fori_loop(0, n, fill_table, 0)
    weight_hop(0)
    dispatch(9, 1, dm, sx_m, rx_m)
    ring_p.rest(2, product_p(2))
    ring_p.second(2)
    for i in range(1, BLOCKS):
        ordered(send_ids, spans[i], w_send)
        first_hop(i)
    for i in range(BLOCKS):
        ordered(keep_ids, spans[i], w_keep)

    def blend(i):
        landed(5 + i, w_got.at[:, pl.ds(0, (n - 1) * piece), spans[i]])

        @pl.loop(0, 3 * (width // 128))
        def _(tile):
            q, rows = lax.div(tile, width // 128), block(lax.rem(tile, width // 128), 128)
            both = w_keep[q, rows, spans[i]].astype(F32) + w_got[q, rows, spans[i]].astype(F32)
            w_keep[q, rows, spans[i]] = (0.5 * both).astype(BF)

    def gradient(left, full, rows, q, store):
        tile_n = 256

        @pl.loop(0, width // tile_n)
        def _(tile):
            right = full[q].reshape(rows, full.shape[3])
            store(tile, mm_tn(left[:, block(tile, tile_n)], right).astype(BF))

    def grads_p(q, target):
        def store(tile, value):
            part_p[target, pl.ds(tile * 2, 2)] = value.reshape(2, 128, neurons)

        gradient(rx_p.at[1 if q == 0 else 0], full_p, rows_p, q, store)
        pltpu.make_async_copy(part_p.at[target], out_p.at[target], out_s.at[target]).start()

    halves = pl.ds(0, 2)
    jobs = []

    def put(src, dst):
        copy = pltpu.make_async_copy(src, dst, out_s.at[3 + len(jobs)])
        copy.start()
        jobs.append(copy)

    def grads_m(i, q, target):
        part = blocks[i].part

        def store(tile, value):
            part[target, tile] = value

        gradient(rx_m.at[1 if q == 0 else 0], blocks[i].full, rows_m, q, store)

    def grad_hop(i):
        part, mid = blocks[i].part, g_mid[i]
        size = pl.ds(cut[i], cols - cut[i])

        def src(d):
            return part.at[:, lax.div(d, n // 2), block(lax.rem(d, n // 2), piece), size]

        scatter(10 + i, src, lambda m: mid.at[m])
        mid[me] = part[:, lax.div(me, n // 2), block(lax.rem(me, n // 2), piece), size]
        for q in range(3):
            put(part.at[q, halves], out_m.at[q, :, :, spans[i]])

    def back_hop(i):
        far, size = g_far[i], pl.ds(spans[i].start, cols - cut[i])
        left_here(5 + i, w_mid[i].at[peers])

        def dst(m):
            return far.at[:, lax.div(m, n // 2), block(lax.rem(m, n // 2), piece), :]

        second_hop(10 + i, 13 + i, g_mid[i], size, dst)
        rows = block(lax.rem(me, n // 2), piece)
        far[:, lax.div(me, n // 2), rows, :] = w_send[:, block(me, piece), size]

    unit = lax.broadcasted_iota(jnp.int32, (1, cols), 1)
    cover = jnp.where((unit < skip) & (is_src > 0), 0.0, 1.0).astype(F32)

    def mix_outputs():
        landed(16, back_p.at[all_p])
        landed(17, back_m.at[all_m])
        span_p, span_m = pl.ds(0, rows_p), pl.ds(rows_p, rows_m)
        total = mm(place_hi[:, span_p], back_p[...]) + mm(place_lo[:, span_p], back_p[...])
        total += mm(place_hi[:, span_m], back_m[...]) + mm(place_lo[:, span_m], back_m[...])
        mixed[...] = total.astype(BF)

    def enter(i):
        blend(i)
        for q in range(3):
            blocks[i].start(q, product_m(i, q))

    def rest(i):
        for q in range(3):
            blocks[i].rest(q, product_m(i, q))

    def seconds(i):
        for q in range(3):
            blocks[i].second(q)

    def publish(i):
        blocks[i].acts(cover if cut[i] else None)
        for q in range(3):
            blocks[i].publish(q)

    def forwards(i):
        for q in range(3):
            blocks[i].forward(q)

    def leave(i):
        blocks[i].sent((0, 1, 2, 3))
        for q, target in ((0, 2), (1, 0), (2, 1)):
            blocks[i].arrived(q)
            grads_m(i, q, target)
        grad_hop(i)

    def outputs_p():
        ring_p.arrived(0)
        left_here(0, sx_p.at[0, all_p])
        for index in range(N_HID):
            rows = pl.ds(index * ring_p.chunk, ring_p.chunk)
            sx_p[0, rows] = mm_nt(full_p[0, index], weights[2, 1 - slot]).astype(BF)
        scatter(16, lambda d: sx_p.at[0, block(d, dp)], lambda m: back_p.at[block(m, dp)])
        back_p[block(me, dp)] = sx_p[0, block(me, dp)]

    def outputs_m():
        for i in range(BLOCKS):
            blocks[i].arrived(0)
        left_here(8, sx_m.at[0, all_m])
        for index in range(N_HID):
            rows = pl.ds(index * blocks[0].chunk, blocks[0].chunk)
            value = mm_nt(blocks[0].full[0, index], w_keep[2, :, spans[0]])
            for i in range(1, BLOCKS):
                value += mm_nt(blocks[i].full[0, index], w_keep[2, :, spans[i]])
            sx_m[0, rows] = value.astype(BF)
        scatter(17, lambda d: sx_m.at[0, block(d, dm)], lambda m: back_m.at[block(m, dm)])
        back_m[block(me, dm)] = sx_m[0, block(me, dm)]

    landed(8, rx_m.at[0, all_m])
    blend(0)
    blocks[0].start(0, product_m(0, 0))
    blocks[0].start(1, product_m(0, 1))
    ring_p.acts(None)
    ring_p.publish(0)
    blocks[0].rest(0, product_m(0, 0))
    blocks[0].second(0)
    blocks[0].rest(1, product_m(0, 1))
    blocks[0].second(1)
    landed(9, rx_m.at[1, all_m])
    blocks[0].start(2, product_m(0, 2))
    blocks[0].rest(2, product_m(0, 2))
    weight_hop(1)
    blocks[0].second(2)
    ring_p.forward(0)
    publish(0)
    weight_hop(2)
    enter(1)
    rest(1)
    forwards(0)
    outputs_p()
    enter(2)
    seconds(1)
    rest(2)
    leave(0)
    publish(1)
    seconds(2)
    back_hop(0)
    forwards(1)
    publish(2)
    leave(1)
    forwards(2)
    ring_p.publish(1)
    ring_p.publish(2)
    ring_p.sent((0, 1, 2, 3))
    leave(2)
    back_hop(1)
    outputs_m()
    ring_p.forward(1)
    back_hop(2)
    ring_p.forward(2)
    grads_p(0, 2)
    ring_p.arrived(1)
    grads_p(1, 0)
    ring_p.arrived(2)
    grads_p(2, 1)

    for i in range(BLOCKS):
        if i == BLOCKS - 1:
            mix_outputs()
        landed(13 + i, g_mid[i].at[peers])
        for q in range(3):
            put(g_far[i].at[q], out_m.at[q, :, :, pl.ds(tail + spans[i].start + cut[i], cols - cut[i])])

    left_here(1, sx_p.at[1, all_p])
    left_here(9, sx_m.at[1, all_m])
    left_here(16, sx_p.at[0, all_p])
    left_here(17, sx_m.at[0, all_m])
    for i in range(BLOCKS):
        left_here(13 + i, g_mid[i].at[peers])
    for ring in rings:
        ring.sent((4, 5, 6, 7))
    for q in range(3):
        pltpu.make_async_copy(part_p.at[q], out_p.at[q], out_s.at[q]).wait()
    for job in jobs:
        job.wait()


def mega(sources, targets, perm, routing, route_w, tokens, cot, gate, up, down, n, depth):
    width, neurons = gate.shape[1], gate.shape[2]
    half = -(-neurons // 256) * 128
    far = neurons - half
    cols = half // BLOCKS
    fars = [cols] * (BLOCKS - 1) + [far - (BLOCKS - 1) * cols]
    rows_p, rows_m = n * depth, 2 * n * depth
    piece = width // n
    cp, cm = rows_p // N_HID, rows_m // N_HID
    vmem = pl.BlockSpec(memory_space=pltpu.VMEM)
    smem = pl.BlockSpec(memory_space=pltpu.SMEM)
    hbm = pl.BlockSpec(memory_space=pl.ANY)

    def ring(chunk, cols):
        return [
            pltpu.VMEM((3, N_HID, chunk, cols), BF),
            pltpu.VMEM((3, chunk // 2, cols), BF),
            pltpu.VMEM((3, chunk // 2, cols), BF),
            pltpu.VMEM((3, chunk, cols), BF),
            pltpu.VMEM((3, chunk, cols), BF),
            pltpu.VMEM((3, N_HID, chunk, cols), BF),
        ]

    return pl.pallas_call(
        mega_kernel,
        out_shape=(
            jax.ShapeDtypeStruct(tokens.shape, BF),
            jax.ShapeDtypeStruct((1,), jnp.int32),
            jax.ShapeDtypeStruct((3, width // 128, 128, neurons), BF),
            jax.ShapeDtypeStruct((3, 2, width // 2, neurons), BF),
        ),
        in_specs=[smem] * 2 + [vmem] * 5 + [hbm] * 3,
        out_specs=(vmem, smem, hbm, hbm),
        scratch_shapes=[
            pltpu.SMEM((n,), jnp.int32),
            pltpu.VMEM((3, *gate.shape), BF),
            pltpu.VMEM((2, 8, tokens.shape[0]), F32),
            *[pltpu.VMEM((tokens.shape[0], rows_p + rows_m), BF)] * 3,
            pltpu.VMEM((neurons, cols), BF),
            pltpu.VMEM((2, rows_p, width), BF),
            pltpu.VMEM((2, rows_m, width), BF),
            pltpu.VMEM((2, rows_p, width), BF),
            pltpu.VMEM((2, rows_m, width), BF),
            *[pltpu.VMEM((3, width, half), BF)] * 3,
            pltpu.VMEM((rows_p, width), BF),
            pltpu.VMEM((rows_m, width), BF),
            *[pltpu.VMEM((n, 3, piece, cols), BF)] * BLOCKS,
            *[pltpu.VMEM((n, 3, piece, size), BF) for size in fars],
            *[pltpu.VMEM((3, 2, width // 2, size), BF) for size in fars],
            *ring(cp, neurons),
            *(ring(cm, cols) * BLOCKS),
            pltpu.SemaphoreType.DMA((2 + 2 * BLOCKS, 8, 3)),
            pltpu.SemaphoreType.DMA((18,)),
            pltpu.SemaphoreType.DMA((18,)),
            pltpu.SemaphoreType.DMA((3,)),
            pltpu.SemaphoreType.DMA((3 + 6 * BLOCKS,)),
        ],
        compiler_params=pltpu.CompilerParams(
            collective_id=0, has_side_effects=True, vmem_limit_bytes=67_043_328
        ),
    )(sources, targets, perm, routing, route_w, tokens, cot, gate, up, down)


def shards(
    tokens,
    cotangent,
    gate_weight,
    up_weight,
    down_weight,
    routing,
    route_weight,
    merge_source,
    merge_target,
    neuron_perm,
):
    devices_n = lax.axis_size("expert")
    exp_local, width, neurons = gate_weight.shape
    tok_local, top_count = routing.shape
    depth = max(2, tok_local * top_count * 4 // (3 * exp_local * devices_n))
    mixed, role, grads_p, grads_m = mega(
        merge_source,
        merge_target,
        neuron_perm,
        routing.T,
        route_weight.T,
        tokens,
        cotangent,
        gate_weight,
        up_weight,
        down_weight,
        devices_n,
        depth,
    )
    grads_p = grads_p.reshape(3, width, neurons)
    grads_m = grads_m.reshape(3, width, neurons)

    role = role[0]
    place = jnp.arange(exp_local, dtype=jnp.int32)[:, None, None]
    is_merge = place == role % 2

    def final(q):
        merged = jnp.where(role >= 2, jnp.zeros((), BF), grads_m[q][None])
        return jnp.where(is_merge, merged, grads_p[q][None])

    return (mixed, final(0), final(1), final(2))


def solution(mesh):
    placed = (
        P("expert", "hidden"),
        P("expert", "hidden"),
        P("expert", "hidden", None),
        P("expert", "hidden", None),
        P("expert", "hidden", None),
        P("expert", None),
        P("expert", None),
        P(),
        P(),
        P(),
    )
    return jax.shard_map(
        shards,
        mesh=mesh,
        in_specs=placed,
        out_specs=(
            P("expert", "hidden"),
            P("expert", "hidden", None),
            P("expert", "hidden", None),
            P("expert", "hidden", None),
        ),
        check_vma=False,
    )
```

```python
import jax
import jax.numpy as jnp
from jax import lax
from jax.experimental import pallas as pl
from jax.experimental.pallas import tpu as pltpu
from jax.sharding import PartitionSpec as P

BF = jnp.bfloat16
F32 = jnp.float32
MESH = pl.DeviceIdType.MESH
N_HID = 4
BLOCKS = 3


def silu_parts(values):
    sigma = jax.nn.sigmoid(values)
    return (values * sigma, sigma * (1.0 + values * (1.0 - sigma)))


def mm(a, b):
    return jnp.dot(a, b, preferred_element_type=F32)


def mm_nt(a, b):
    return lax.dot_general(a, b, (((1,), (1,)), ((), ())), preferred_element_type=F32)


def mm_tn(a, b):
    return lax.dot_general(a, b, (((0,), (0,)), ((), ())), preferred_element_type=F32)


def add_to(ref, other):
    ref[...] = (ref[...].astype(F32) + other[...].astype(F32)).astype(BF)


class Ring:
    def __init__(self, part, in_a, in_b, in_l, in_r, full, sends, recvs):
        self.part, self.in_a, self.in_b, self.in_l, self.in_r = part, in_a, in_b, in_l, in_r
        self.full, self.sends, self.recvs = full, sends, recvs
        self.me = lax.axis_index("hidden")
        self.right = lax.rem(self.me + 1, N_HID)
        self.left = lax.rem(self.me + 3, N_HID)
        self.across = lax.rem(self.me + 2, N_HID)
        self.chunk = part.shape[2]
        self.lo = pl.ds(0, self.chunk // 2)
        self.hi = pl.ds(self.chunk // 2, self.chunk // 2)
        self.copies = {}
        self.seen = set()

    def send(self, src, dst, kind, q, peer):
        copy = pltpu.make_async_remote_copy(
            src_ref=src,
            dst_ref=dst,
            send_sem=self.sends.at[kind, q],
            recv_sem=self.recvs.at[kind, q],
            device_id={"hidden": peer},
            device_id_type=MESH,
        )
        copy.start()
        self.copies[kind, q] = copy

    def start(self, q, product):
        part = self.part
        part[q, self.across] = product(self.across).astype(BF)
        self.send(part.at[q, self.across, self.lo], self.in_a.at[q], 0, q, self.right)
        self.send(part.at[q, self.across, self.hi], self.in_b.at[q], 1, q, self.left)

    def rest(self, q, product):
        for index in (self.right, self.left, self.me):
            self.part[q, index] = product(index).astype(BF)

    def second(self, q):
        part = self.part
        self.copies[0, q].wait_recv()
        add_to(part.at[q, self.right, self.lo], self.in_a.at[q])
        self.send(part.at[q, self.right], self.in_l.at[q], 2, q, self.right)
        self.copies[1, q].wait_recv()
        add_to(part.at[q, self.left, self.hi], self.in_b.at[q])
        self.send(part.at[q, self.left], self.in_r.at[q], 3, q, self.left)

    def acts(self, cover):
        for q in range(3):
            self.copies[2, q].wait_recv()
            self.copies[3, q].wait_recv()
        step = 32

        @pl.loop(0, self.chunk // step)
        def _(tile):
            rows = pl.ds(pl.multiple_of(tile * step, step), step)

            def total(q):
                own = self.part[q, self.me, rows].astype(F32)
                return own + self.in_l[q, rows].astype(F32) + self.in_r[q, rows].astype(F32)

            g, u, dh = total(0), total(1), total(2)
            active, slope = silu_parts(g)
            values = (active * u, dh * u * slope, dh * active)
            for q in range(3):
                value = values[q] if cover is None else values[q] * cover
                self.full[q, self.me, rows] = value.astype(BF)

    def publish(self, q):
        mine = self.full.at[q, self.me]
        self.send(mine, mine, 4, q, self.right)
        self.send(mine, mine, 5, q, self.left)

    def forward(self, q):
        self.copies[4, q].wait_recv()
        half = self.full.at[q, self.left, self.lo]
        self.send(half, half, 6, q, self.right)
        self.copies[5, q].wait_recv()
        half = self.full.at[q, self.right, self.hi]
        self.send(half, half, 7, q, self.left)

    def arrived(self, q):
        for kind in (6, 7):
            if (kind, q) not in self.seen:
                self.seen.add((kind, q))
                self.copies[kind, q].wait_recv()

    def sent(self, kinds):
        for kind in kinds:
            for q in range(3):
                self.copies[kind, q].wait_send()


def mega_kernel(
    sources,
    targets,
    perm_ref,
    routing,
    route_w,
    tokens,
    cot,
    gate_hbm,
    up_hbm,
    down_hbm,
    mixed,
    marks,
    *rest_refs,
):
    out_p, out_m, scratch = rest_refs[:3], rest_refs[3:6], list(rest_refs[6:])

    def take(count):
        got = scratch[:count]
        del scratch[:count]
        return got

    table, weights, columns, place, place_hi, place_lo, hot, sx_p, sx_m, rx_p, rx_m = take(11)
    w_send, w_got, w_keep, back_p, back_m = take(5)
    w_mid, g_mid, g_far = take(BLOCKS), take(BLOCKS), take(BLOCKS)
    scraps = [take(6) for _ in range(1 + BLOCKS)]
    ring_sems, a2a_s, a2a_r, in_s, out_s = take(5)
    n = lax.axis_size("expert")
    me = lax.axis_index("expert")
    width = tokens.shape[1]
    top, tok_n = routing.shape
    neurons = weights.shape[3]
    half = w_keep.shape[2]
    tail = neurons - half
    cols = half // BLOCKS
    skip = 2 * half - neurons
    piece = width // n
    rows_p, rows_m = sx_p.shape[1], sx_m.shape[1]
    dp, dm = rows_p // n, rows_m // n
    log_dp = dp.bit_length() - 1
    spans = [pl.ds((i + 1) % BLOCKS * cols, cols) for i in range(BLOCKS)]
    cut = [0] * (BLOCKS - 1) + [skip]

    def block(index, size):
        return pl.ds(pl.multiple_of(index * size, size), size)

    loads = []
    for q, ref in enumerate((gate_hbm, up_hbm, down_hbm)):
        loads.append(pltpu.make_async_copy(ref, weights.at[q], in_s.at[q]))
        loads[q].start()

    def peer(step):
        nodes = n // 2
        side = 4 if nodes == 16 else nodes
        core, node = lax.rem(me, 2), lax.div(me, 2)
        flip, shift = lax.rem(step, 2), lax.div(step, 2)
        hi = lax.rem(lax.div(node, side) + lax.div(shift, side), nodes // side)
        lo = lax.rem(lax.rem(node, side) + lax.rem(shift, side), side)
        return (hi * side + lo) * 2 + lax.rem(core + flip, 2)

    rings = [Ring(*scraps[i], ring_sems.at[2 * i], ring_sems.at[2 * i + 1]) for i in range(1 + BLOCKS)]
    ring_p, blocks = rings[0], rings[1:]
    part_p, full_p = ring_p.part, ring_p.full

    barrier = pltpu.get_barrier_semaphore()
    for other in (ring_p.left, ring_p.right):
        pl.semaphore_signal(barrier, inc=1, device_id={"hidden": other}, device_id_type=MESH)

    @pl.loop(1, n)
    def _(step):
        pl.semaphore_signal(barrier, inc=1, device_id={"expert": peer(step)}, device_id_type=MESH)

    columns[...] = jnp.zeros_like(columns)
    columns[0, 0:top] = routing[...].astype(F32)
    columns[1, 0:top] = route_w[...]
    names, shares = jnp.transpose(columns[0]), jnp.transpose(columns[1])

    pairs = sources.shape[0]
    wide = rows_p
    log_wide = log_dp

    def make_place(tile):
        lane = lax.broadcasted_iota(jnp.int32, (8, wide), 1)
        if tile == 0:
            device = lax.shift_right_logical(lane, log_dp)
        else:
            lane = lane + (tile - 1) * wide
            device = lax.shift_right_logical(lane, log_dp + 1)
        source = jnp.zeros((8, wide), jnp.int32)
        target = jnp.zeros((8, wide), jnp.int32)
        own = jnp.zeros((8, wide), jnp.int32)
        for m in range(pairs):
            s, t = sources[m], targets[m]
            at_s, at_t = device == lax.shift_right_logical(s, 1), device == lax.shift_right_logical(t, 1)
            source = jnp.where(at_s | at_t, s, source)
            target = jnp.where(at_s | at_t, t, target)
            own = jnp.where(at_s, s, jnp.where(at_t, t, own))
        if tile == 0:
            expert = device * 4 + 1 - own
        else:
            is_target = (lax.shift_right_logical(lane, log_dp) & 1) == 0
            expert = jnp.where(is_target, target, source)
        expert = expert[0:1, :]
        chosen = jnp.zeros((tok_n, wide), F32)
        weight = jnp.zeros((tok_n, wide), F32)
        expert = expert.astype(F32)
        for k in range(top):
            hit = names[:, k : k + 1] == expert
            chosen = jnp.where(hit, 1.0, chosen)
            weight = jnp.where(hit, shares[:, k : k + 1], weight)
        row = lax.broadcasted_iota(jnp.int32, (tok_n, tok_n), 0)
        col = lax.broadcasted_iota(jnp.int32, (tok_n, tok_n), 1)
        before = jnp.where(col < row, 1.0, 0.0).astype(BF)
        rank = mm(before, chosen.astype(BF))
        slot_of = (lane[0:1, :] & (dp - 1)).astype(F32)
        here = (rank == slot_of) & (chosen > 0.5)
        hi = weight.astype(BF).astype(F32)
        span = pl.ds(tile * wide, wide)
        place[:, span] = jnp.where(here, 1.0, 0.0).astype(BF)
        place_hi[:, span] = jnp.where(here, hi, 0.0).astype(BF)
        place_lo[:, span] = jnp.where(here, weight - hi, 0.0).astype(BF)

    def build_x(base, rows, out):
        @pl.loop(0, rows // 128)
        def _(tile):
            src = pl.ds(pl.multiple_of(base + tile * 128, 128), 128)
            out[0, block(tile, 128)] = mm_tn(place[:, src], tokens[...]).astype(BF)

    def build_dy(base, rows, out):
        @pl.loop(0, rows // 128)
        def _(tile):
            src = pl.ds(pl.multiple_of(base + tile * 128, 128), 128)
            value = mm_tn(place_hi[:, src], cot[...]) + mm_tn(place_lo[:, src], cot[...])
            out[1, block(tile, 128)] = value.astype(BF)

    def scatter(sem, src_of, dst_of):
        @pl.loop(1, n)
        def _(step):
            other = peer(lax.rem(step * 5, n))
            pltpu.make_async_remote_copy(
                src_ref=src_of(other),
                dst_ref=dst_of(me),
                send_sem=a2a_s.at[sem],
                recv_sem=a2a_r.at[sem],
                device_id={"expert": other},
                device_id_type=MESH,
            ).start()

    def landed(sem, ref):
        pltpu.make_async_copy(ref, ref, a2a_r.at[sem]).wait()

    def left_here(sem, ref):
        pltpu.make_async_copy(ref, ref, a2a_s.at[sem]).wait()

    all_p, all_m, peers = pl.ds(0, (n - 1) * dp), pl.ds(0, (n - 1) * dm), pl.ds(0, n - 1)

    def dispatch(sem, which, size, src, dst):
        scatter(sem, lambda d: src.at[which, block(d, size)], lambda m: dst.at[which, block(m, size)])
        dst[which, block(me, size)] = src[which, block(me, size)]

    make_place(0)
    build_x(0, rows_p, sx_p)
    pl.semaphore_wait(barrier, n + 1)
    dispatch(0, 0, dp, sx_p, rx_p)
    build_dy(0, rows_p, sx_p)
    dispatch(1, 1, dp, sx_p, rx_p)

    slot, is_src = jnp.int32(0), jnp.int32(0)
    for m in range(pairs):
        s, t = sources[m], targets[m]
        at_s, at_t = lax.shift_right_logical(s, 1) == me, lax.shift_right_logical(t, 1) == me
        slot = jnp.where(at_s, s & 1, jnp.where(at_t, t & 1, slot))
        is_src = jnp.where(at_s, 1, is_src)
    marks[0:8, :] = jnp.zeros((8, neurons), jnp.int32) + slot
    marks[8:16, :] = jnp.zeros((8, neurons), jnp.int32) + is_src

    def fill_table(device, carry):
        partner = jnp.int32(0)
        for m in range(pairs):
            s, t = lax.shift_right_logical(sources[m], 1), lax.shift_right_logical(targets[m], 1)
            partner = jnp.where(s == device, t, jnp.where(t == device, s, partner))
        table[device] = partner
        return carry

    perm = jnp.zeros((8, neurons), jnp.int32)
    for m in range(pairs):
        s, t = lax.shift_right_logical(sources[m], 1), lax.shift_right_logical(targets[m], 1)
        mine = jnp.where((s == me) | (t == me), 1, 0)
        perm = perm + perm_ref[m : m + 1, :] * mine
    perm = perm[0:1, :]
    lane = lax.broadcasted_iota(jnp.int32, (1, half), 1)
    send_ids = jnp.where(is_src > 0, perm[:, :half], lane + tail)
    keep_ids = jnp.where(is_src > 0, perm[:, tail:], lane)

    def ordered(ids, span, out):
        units = ids[:, span.start : span.start + span.size]

        @pl.loop(0, neurons // 128)
        def _(tile):
            rows = lax.broadcasted_iota(jnp.int32, (128, span.size), 0) + tile * 128
            hot[block(tile, 128)] = jnp.where(rows == units, 1.0, 0.0).astype(BF)

        @pl.loop(0, 3)
        def _(q):
            out[q, :, span] = mm(weights[q, slot], hot[...]).astype(BF)

    def first_hop(i):
        scatter(2 + i, lambda d: w_send.at[:, block(d, piece), spans[i]], lambda m: w_mid[i].at[m])
        w_mid[i][me] = w_send[:, block(me, piece), spans[i]]

    def second_hop(first, then, mid, span, dst_of):
        landed(first, mid.at[peers])
        left_here(first, mid.at[peers])

        @pl.loop(0, n)
        def _(other):
            w_send[:, block(other, piece), span] = mid[table[other]]

        scatter(then, lambda d: w_send.at[:, block(d, piece), span], dst_of)

    def weight_hop(i):
        second_hop(2 + i, 5 + i, w_mid[i], spans[i], lambda m: w_got.at[:, block(m, piece), spans[i]])
        w_got[:, block(me, piece), spans[i]] = w_send[:, block(me, piece), spans[i]]

    for load in loads:
        load.wait()
    ordered(send_ids, spans[0], w_send)
    first_hop(0)
    make_place(1)
    make_place(2)
    build_x(rows_p, rows_m, sx_m)
    dispatch(8, 0, dm, sx_m, rx_m)

    lefts = (0, 0, 1)

    def product_p(q):
        def product(index):
            return mm(rx_p[lefts[q], block(index, ring_p.chunk), :], weights[q, 1 - slot])

        return product

    def product_m(i, q):
        def product(index):
            return mm(rx_m[lefts[q], block(index, blocks[i].chunk), :], w_keep[q, :, spans[i]])

        return product

    landed(0, rx_p.at[0, all_p])
    ring_p.start(0, product_p(0))
    ring_p.start(1, product_p(1))
    build_dy(rows_p, rows_m, sx_m)
    landed(1, rx_p.at[1, all_p])
    ring_p.start(2, product_p(2))
    ring_p.rest(0, product_p(0))
    ring_p.second(0)
    ring_p.rest(1, product_p(1))
    ring_p.second(1)
    lax.fori_loop(0, n, fill_table, 0)
    weight_hop(0)
    dispatch(9, 1, dm, sx_m, rx_m)
    ring_p.rest(2, product_p(2))
    ring_p.second(2)
    for i in range(1, BLOCKS):
        ordered(send_ids, spans[i], w_send)
        first_hop(i)
    for i in range(BLOCKS):
        ordered(keep_ids, spans[i], w_keep)

    def blend(i):
        landed(5 + i, w_got.at[:, pl.ds(0, (n - 1) * piece), spans[i]])

        @pl.loop(0, 3 * (width // 128))
        def _(tile):
            q, rows = lax.div(tile, width // 128), block(lax.rem(tile, width // 128), 128)
            both = w_keep[q, rows, spans[i]].astype(F32) + w_got[q, rows, spans[i]].astype(F32)
            w_keep[q, rows, spans[i]] = (0.5 * both).astype(BF)

    def gradient(left, full, rows, q, store):
        tile_n = 256

        @pl.loop(0, width // tile_n)
        def _(tile):
            right = full[q].reshape(rows, full.shape[3])
            store(tile, mm_tn(left[:, block(tile, tile_n)], right).astype(BF))

    def grads_p(q, target):
        def store(tile, value):
            part_p[target, pl.ds(tile * 2, 2)] = value.reshape(2, 128, neurons)

        gradient(rx_p.at[1 if q == 0 else 0], full_p, rows_p, q, store)
        pltpu.make_async_copy(part_p.at[target], out_p[target], out_s.at[target]).start()

    halves = pl.ds(0, 2)
    jobs = []

    def put(src, dst):
        copy = pltpu.make_async_copy(src, dst, out_s.at[3 + len(jobs)])
        copy.start()
        jobs.append(copy)

    def grads_m(i, q, target):
        part = blocks[i].part

        def store(tile, value):
            part[target, tile] = value

        gradient(rx_m.at[1 if q == 0 else 0], blocks[i].full, rows_m, q, store)

    def grad_hop(i):
        part, mid = blocks[i].part, g_mid[i]
        size = pl.ds(cut[i], cols - cut[i])

        def src(d):
            return part.at[:, lax.div(d, n // 2), block(lax.rem(d, n // 2), piece), size]

        scatter(10 + i, src, lambda m: mid.at[m])
        mid[me] = part[:, lax.div(me, n // 2), block(lax.rem(me, n // 2), piece), size]
        for q in range(3):
            put(part.at[q, halves], out_m[q].at[:, :, spans[i]])

    def back_hop(i):
        far, size = g_far[i], pl.ds(spans[i].start, cols - cut[i])
        left_here(5 + i, w_mid[i].at[peers])

        def dst(m):
            return far.at[:, lax.div(m, n // 2), block(lax.rem(m, n // 2), piece), :]

        second_hop(10 + i, 13 + i, g_mid[i], size, dst)
        rows = block(lax.rem(me, n // 2), piece)
        far[:, lax.div(me, n // 2), rows, :] = w_send[:, block(me, piece), size]

    unit = lax.broadcasted_iota(jnp.int32, (1, cols), 1)
    cover = jnp.where((unit < skip) & (is_src > 0), 0.0, 1.0).astype(F32)

    def mix_outputs():
        landed(16, back_p.at[all_p])
        landed(17, back_m.at[all_m])
        span_p, span_m = pl.ds(0, rows_p), pl.ds(rows_p, rows_m)
        total = mm(place_hi[:, span_p], back_p[...]) + mm(place_lo[:, span_p], back_p[...])
        total += mm(place_hi[:, span_m], back_m[...]) + mm(place_lo[:, span_m], back_m[...])
        mixed[...] = total.astype(BF)

    def enter(i):
        blend(i)
        for q in range(3):
            blocks[i].start(q, product_m(i, q))

    def rest(i):
        for q in range(3):
            blocks[i].rest(q, product_m(i, q))

    def seconds(i):
        for q in range(3):
            blocks[i].second(q)

    def publish(i):
        blocks[i].acts(cover if cut[i] else None)
        for q in range(3):
            blocks[i].publish(q)

    def forwards(i):
        for q in range(3):
            blocks[i].forward(q)

    def leave(i):
        blocks[i].sent((0, 1, 2, 3))
        for q, target in ((0, 2), (1, 0), (2, 1)):
            blocks[i].arrived(q)
            grads_m(i, q, target)
        grad_hop(i)

    def outputs_p():
        ring_p.arrived(0)
        left_here(0, sx_p.at[0, all_p])
        for index in range(N_HID):
            rows = pl.ds(index * ring_p.chunk, ring_p.chunk)
            sx_p[0, rows] = mm_nt(full_p[0, index], weights[2, 1 - slot]).astype(BF)
        scatter(16, lambda d: sx_p.at[0, block(d, dp)], lambda m: back_p.at[block(m, dp)])
        back_p[block(me, dp)] = sx_p[0, block(me, dp)]

    def outputs_m():
        for i in range(BLOCKS):
            blocks[i].arrived(0)
        left_here(8, sx_m.at[0, all_m])
        for index in range(N_HID):
            rows = pl.ds(index * blocks[0].chunk, blocks[0].chunk)
            value = mm_nt(blocks[0].full[0, index], w_keep[2, :, spans[0]])
            for i in range(1, BLOCKS):
                value += mm_nt(blocks[i].full[0, index], w_keep[2, :, spans[i]])
            sx_m[0, rows] = value.astype(BF)
        scatter(17, lambda d: sx_m.at[0, block(d, dm)], lambda m: back_m.at[block(m, dm)])
        back_m[block(me, dm)] = sx_m[0, block(me, dm)]

    landed(8, rx_m.at[0, all_m])
    blend(0)
    blocks[0].start(0, product_m(0, 0))
    blocks[0].start(1, product_m(0, 1))
    ring_p.acts(None)
    ring_p.publish(0)
    blocks[0].rest(0, product_m(0, 0))
    blocks[0].second(0)
    blocks[0].rest(1, product_m(0, 1))
    blocks[0].second(1)
    landed(9, rx_m.at[1, all_m])
    blocks[0].start(2, product_m(0, 2))
    blocks[0].rest(2, product_m(0, 2))
    weight_hop(1)
    blocks[0].second(2)
    ring_p.forward(0)
    publish(0)
    weight_hop(2)
    enter(1)
    rest(1)
    forwards(0)
    outputs_p()
    enter(2)
    seconds(1)
    rest(2)
    leave(0)
    publish(1)
    seconds(2)
    back_hop(0)
    forwards(1)
    publish(2)
    leave(1)
    forwards(2)
    ring_p.publish(1)
    ring_p.publish(2)
    ring_p.sent((0, 1, 2, 3))
    leave(2)
    back_hop(1)
    outputs_m()
    ring_p.forward(1)
    back_hop(2)
    ring_p.forward(2)
    grads_p(0, 2)
    ring_p.arrived(1)
    grads_p(1, 0)
    ring_p.arrived(2)
    grads_p(2, 1)

    for i in range(BLOCKS):
        if i == BLOCKS - 1:
            mix_outputs()
        landed(13 + i, g_mid[i].at[peers])
        for q in range(3):
            put(g_far[i].at[q], out_m[q].at[:, :, pl.ds(tail + spans[i].start + cut[i], cols - cut[i])])

    left_here(1, sx_p.at[1, all_p])
    left_here(9, sx_m.at[1, all_m])
    left_here(16, sx_p.at[0, all_p])
    left_here(17, sx_m.at[0, all_m])
    for i in range(BLOCKS):
        left_here(13 + i, g_mid[i].at[peers])
    for ring in rings:
        ring.sent((4, 5, 6, 7))
    for q in range(3):
        pltpu.make_async_copy(part_p.at[q], out_p[q], out_s.at[q]).wait()
    for job in jobs:
        job.wait()


def mega(sources, targets, perm, routing, route_w, tokens, cot, gate, up, down, n, depth):
    width, neurons = gate.shape[1], gate.shape[2]
    half = -(-neurons // 256) * 128
    far = neurons - half
    cols = half // BLOCKS
    fars = [cols] * (BLOCKS - 1) + [far - (BLOCKS - 1) * cols]
    rows_p, rows_m = n * depth, 2 * n * depth
    piece = width // n
    cp, cm = rows_p // N_HID, rows_m // N_HID
    vmem = pl.BlockSpec(memory_space=pltpu.VMEM)
    smem = pl.BlockSpec(memory_space=pltpu.SMEM)
    hbm = pl.BlockSpec(memory_space=pl.ANY)

    def ring(chunk, cols):
        return [
            pltpu.VMEM((3, N_HID, chunk, cols), BF),
            pltpu.VMEM((3, chunk // 2, cols), BF),
            pltpu.VMEM((3, chunk // 2, cols), BF),
            pltpu.VMEM((3, chunk, cols), BF),
            pltpu.VMEM((3, chunk, cols), BF),
            pltpu.VMEM((3, N_HID, chunk, cols), BF),
        ]

    return pl.pallas_call(
        mega_kernel,
        out_shape=(
            jax.ShapeDtypeStruct(tokens.shape, BF),
            jax.ShapeDtypeStruct((16, neurons), jnp.int32),
            *[jax.ShapeDtypeStruct((width // 128, 128, neurons), BF)] * 3,
            *[jax.ShapeDtypeStruct((2, width // 2, neurons), BF)] * 3,
        ),
        in_specs=[smem] * 2 + [vmem] * 5 + [hbm] * 3,
        out_specs=(vmem, vmem, *[hbm] * 6),
        scratch_shapes=[
            pltpu.SMEM((n,), jnp.int32),
            pltpu.VMEM((3, *gate.shape), BF),
            pltpu.VMEM((2, 8, tokens.shape[0]), F32),
            *[pltpu.VMEM((tokens.shape[0], rows_p + rows_m), BF)] * 3,
            pltpu.VMEM((neurons, cols), BF),
            pltpu.VMEM((2, rows_p, width), BF),
            pltpu.VMEM((2, rows_m, width), BF),
            pltpu.VMEM((2, rows_p, width), BF),
            pltpu.VMEM((2, rows_m, width), BF),
            *[pltpu.VMEM((3, width, half), BF)] * 3,
            pltpu.VMEM((rows_p, width), BF),
            pltpu.VMEM((rows_m, width), BF),
            *[pltpu.VMEM((n, 3, piece, cols), BF)] * BLOCKS,
            *[pltpu.VMEM((n, 3, piece, size), BF) for size in fars],
            *[pltpu.VMEM((3, 2, width // 2, size), BF) for size in fars],
            *ring(cp, neurons),
            *(ring(cm, cols) * BLOCKS),
            pltpu.SemaphoreType.DMA((2 + 2 * BLOCKS, 8, 3)),
            pltpu.SemaphoreType.DMA((18,)),
            pltpu.SemaphoreType.DMA((18,)),
            pltpu.SemaphoreType.DMA((3,)),
            pltpu.SemaphoreType.DMA((3 + 6 * BLOCKS,)),
        ],
        compiler_params=pltpu.CompilerParams(
            collective_id=0, has_side_effects=True, vmem_limit_bytes=67_043_328
        ),
    )(sources, targets, perm, routing, route_w, tokens, cot, gate, up, down)


def shards(
    tokens,
    cotangent,
    gate_weight,
    up_weight,
    down_weight,
    routing,
    route_weight,
    merge_source,
    merge_target,
    neuron_perm,
):
    devices_n = lax.axis_size("expert")
    exp_local, width, neurons = gate_weight.shape
    tok_local, top_count = routing.shape
    depth = max(2, tok_local * top_count * 4 // (3 * exp_local * devices_n))
    mixed, marks, *grads = mega(
        merge_source,
        merge_target,
        neuron_perm,
        routing.T,
        route_weight.T,
        tokens,
        cotangent,
        gate_weight,
        up_weight,
        down_weight,
        devices_n,
        depth,
    )
    slot, is_source = marks[0][None, None, :], marks[8][None, None, :] > 0
    is_merge = jnp.arange(exp_local, dtype=jnp.int32)[:, None, None] == slot

    def final(q):
        plain = grads[q].reshape(1, width, neurons)
        merged = grads[3 + q].reshape(1, width, neurons)
        rest = jnp.where(is_merge, jnp.zeros((), BF), plain)
        return jnp.where(is_merge & ~is_source, merged, rest)

    return (mixed, final(0), final(1), final(2))


def solution(mesh):
    placed = (
        P("expert", "hidden"),
        P("expert", "hidden"),
        P("expert", "hidden", None),
        P("expert", "hidden", None),
        P("expert", "hidden", None),
        P("expert", None),
        P("expert", None),
        P(),
        P(),
        P(),
    )
    return jax.shard_map(
        shards,
        mesh=mesh,
        in_specs=placed,
        out_specs=(
            P("expert", "hidden"),
            P("expert", "hidden", None),
            P("expert", "hidden", None),
            P("expert", "hidden", None),
        ),
        check_vma=False,
    )
```

```python
import jax
import jax.numpy as jnp
from jax import lax
from jax.experimental import pallas as pl
from jax.experimental.pallas import tpu as pltpu
from jax.sharding import PartitionSpec as P

BF = jnp.bfloat16
F32 = jnp.float32
MESH = pl.DeviceIdType.MESH
N_HID = 4
BLOCKS = 3


def silu_parts(values):
    sigma = jax.nn.sigmoid(values)
    return (values * sigma, sigma * (1.0 + values * (1.0 - sigma)))


def mm(a, b):
    return jnp.dot(a, b, preferred_element_type=F32)


def mm_nt(a, b):
    return lax.dot_general(a, b, (((1,), (1,)), ((), ())), preferred_element_type=F32)


def mm_tn(a, b):
    return lax.dot_general(a, b, (((0,), (0,)), ((), ())), preferred_element_type=F32)


def add_to(ref, other):
    ref[...] = (ref[...].astype(F32) + other[...].astype(F32)).astype(BF)


class Ring:
    def __init__(self, part, in_a, in_b, in_l, in_r, full, sends, recvs):
        self.part, self.in_a, self.in_b, self.in_l, self.in_r = part, in_a, in_b, in_l, in_r
        self.full, self.sends, self.recvs = full, sends, recvs
        self.me = lax.axis_index("hidden")
        self.right = lax.rem(self.me + 1, N_HID)
        self.left = lax.rem(self.me + 3, N_HID)
        self.across = lax.rem(self.me + 2, N_HID)
        self.chunk = part.shape[2]
        self.lo = pl.ds(0, self.chunk // 2)
        self.hi = pl.ds(self.chunk // 2, self.chunk // 2)
        self.copies = {}
        self.seen = set()

    def send(self, src, dst, kind, q, peer):
        copy = pltpu.make_async_remote_copy(
            src_ref=src,
            dst_ref=dst,
            send_sem=self.sends.at[kind, q],
            recv_sem=self.recvs.at[kind, q],
            device_id={"hidden": peer},
            device_id_type=MESH,
        )
        copy.start()
        self.copies[kind, q] = copy

    def start(self, q, product):
        part = self.part
        part[q, self.across] = product(self.across).astype(BF)
        self.send(part.at[q, self.across, self.lo], self.in_a.at[q], 0, q, self.right)
        self.send(part.at[q, self.across, self.hi], self.in_b.at[q], 1, q, self.left)

    def rest(self, q, product):
        for index in (self.right, self.left, self.me):
            self.part[q, index] = product(index).astype(BF)

    def second(self, q):
        part = self.part
        self.copies[0, q].wait_recv()
        add_to(part.at[q, self.right, self.lo], self.in_a.at[q])
        self.send(part.at[q, self.right], self.in_l.at[q], 2, q, self.right)
        self.copies[1, q].wait_recv()
        add_to(part.at[q, self.left, self.hi], self.in_b.at[q])
        self.send(part.at[q, self.left], self.in_r.at[q], 3, q, self.left)

    def acts(self, cover):
        for q in range(3):
            self.copies[2, q].wait_recv()
            self.copies[3, q].wait_recv()
        step = 32

        @pl.loop(0, self.chunk // step)
        def _(tile):
            rows = pl.ds(pl.multiple_of(tile * step, step), step)

            def total(q):
                own = self.part[q, self.me, rows].astype(F32)
                return own + self.in_l[q, rows].astype(F32) + self.in_r[q, rows].astype(F32)

            g, u, dh = total(0), total(1), total(2)
            active, slope = silu_parts(g)
            values = (active * u, dh * u * slope, dh * active)
            for q in range(3):
                value = values[q] if cover is None else values[q] * cover
                self.full[q, self.me, rows] = value.astype(BF)

    def publish(self, q):
        mine = self.full.at[q, self.me]
        self.send(mine, mine, 4, q, self.right)
        self.send(mine, mine, 5, q, self.left)

    def forward(self, q):
        self.copies[4, q].wait_recv()
        half = self.full.at[q, self.left, self.lo]
        self.send(half, half, 6, q, self.right)
        self.copies[5, q].wait_recv()
        half = self.full.at[q, self.right, self.hi]
        self.send(half, half, 7, q, self.left)

    def arrived(self, q):
        for kind in (6, 7):
            if (kind, q) not in self.seen:
                self.seen.add((kind, q))
                self.copies[kind, q].wait_recv()

    def sent(self, kinds):
        for kind in kinds:
            for q in range(3):
                self.copies[kind, q].wait_send()


def mega_kernel(
    sources,
    targets,
    perm_ref,
    routing,
    route_w,
    tokens,
    cot,
    gate_hbm,
    up_hbm,
    down_hbm,
    mixed,
    marks,
    *rest_refs,
):
    out_p, out_m, scratch = rest_refs[:3], rest_refs[3:6], list(rest_refs[6:])

    def take(count):
        got = scratch[:count]
        del scratch[:count]
        return got

    table, weights, columns, place, place_hi, place_lo, hot, sx_p, sx_m, rx_p, rx_m = take(11)
    w_send, w_got, w_keep, back_p, back_m = take(5)
    w_mid, g_mid, g_far = take(BLOCKS), take(BLOCKS), take(BLOCKS)
    scraps = [take(6) for _ in range(1 + BLOCKS)]
    ring_sems, a2a_s, a2a_r, in_s, out_s = take(5)
    n = lax.axis_size("expert")
    me = lax.axis_index("expert")
    width = tokens.shape[1]
    top, tok_n = routing.shape
    neurons = weights.shape[3]
    half = w_keep.shape[2]
    tail = neurons - half
    cols = half // BLOCKS
    skip = 2 * half - neurons
    piece = width // n
    rows_p, rows_m = sx_p.shape[1], sx_m.shape[1]
    dp, dm = rows_p // n, rows_m // n
    log_dp = dp.bit_length() - 1
    spans = [pl.ds((i + 1) % BLOCKS * cols, cols) for i in range(BLOCKS)]
    cut = [0] * (BLOCKS - 1) + [skip]

    def block(index, size):
        return pl.ds(pl.multiple_of(index * size, size), size)

    loads = []
    for q, ref in enumerate((gate_hbm, up_hbm, down_hbm)):
        loads.append(pltpu.make_async_copy(ref, weights.at[q], in_s.at[q]))
        loads[q].start()

    def peer(step):
        nodes = n // 2
        side = 4 if nodes == 16 else nodes
        core, node = lax.rem(me, 2), lax.div(me, 2)
        flip, shift = lax.rem(step, 2), lax.div(step, 2)
        hi = lax.rem(lax.div(node, side) + lax.div(shift, side), nodes // side)
        lo = lax.rem(lax.rem(node, side) + lax.rem(shift, side), side)
        return (hi * side + lo) * 2 + lax.rem(core + flip, 2)

    rings = [Ring(*scraps[i], ring_sems.at[2 * i], ring_sems.at[2 * i + 1]) for i in range(1 + BLOCKS)]
    ring_p, blocks = rings[0], rings[1:]
    part_p, full_p = ring_p.part, ring_p.full

    barrier = pltpu.get_barrier_semaphore()
    for other in (ring_p.left, ring_p.right):
        pl.semaphore_signal(barrier, inc=1, device_id={"hidden": other}, device_id_type=MESH)

    @pl.loop(1, n)
    def _(step):
        pl.semaphore_signal(barrier, inc=1, device_id={"expert": peer(step)}, device_id_type=MESH)

    columns[...] = jnp.zeros_like(columns)
    columns[0, 0:top] = routing[...].astype(F32)
    columns[1, 0:top] = route_w[...]
    names, shares = jnp.transpose(columns[0]), jnp.transpose(columns[1])

    pairs = sources.shape[0]
    wide = rows_p
    log_wide = log_dp

    def make_place(tile):
        lane = lax.broadcasted_iota(jnp.int32, (8, wide), 1)
        if tile == 0:
            device = lax.shift_right_logical(lane, log_dp)
        else:
            lane = lane + (tile - 1) * wide
            device = lax.shift_right_logical(lane, log_dp + 1)
        source = jnp.zeros((8, wide), jnp.int32)
        target = jnp.zeros((8, wide), jnp.int32)
        own = jnp.zeros((8, wide), jnp.int32)
        for m in range(pairs):
            s, t = sources[m], targets[m]
            at_s, at_t = device == lax.shift_right_logical(s, 1), device == lax.shift_right_logical(t, 1)
            source = jnp.where(at_s | at_t, s, source)
            target = jnp.where(at_s | at_t, t, target)
            own = jnp.where(at_s, s, jnp.where(at_t, t, own))
        if tile == 0:
            expert = device * 4 + 1 - own
        else:
            is_target = (lax.shift_right_logical(lane, log_dp) & 1) == 0
            expert = jnp.where(is_target, target, source)
        expert = expert[0:1, :]
        chosen = jnp.zeros((tok_n, wide), F32)
        weight = jnp.zeros((tok_n, wide), F32)
        expert = expert.astype(F32)
        for k in range(top):
            hit = names[:, k : k + 1] == expert
            chosen = jnp.where(hit, 1.0, chosen)
            weight = jnp.where(hit, shares[:, k : k + 1], weight)
        row = lax.broadcasted_iota(jnp.int32, (tok_n, tok_n), 0)
        col = lax.broadcasted_iota(jnp.int32, (tok_n, tok_n), 1)
        before = jnp.where(col < row, 1.0, 0.0).astype(BF)
        rank = mm(before, chosen.astype(BF))
        slot_of = (lane[0:1, :] & (dp - 1)).astype(F32)
        here = (rank == slot_of) & (chosen > 0.5)
        hi = weight.astype(BF).astype(F32)
        span = pl.ds(tile * wide, wide)
        place[:, span] = jnp.where(here, 1.0, 0.0).astype(BF)
        place_hi[:, span] = jnp.where(here, hi, 0.0).astype(BF)
        place_lo[:, span] = jnp.where(here, weight - hi, 0.0).astype(BF)

    def build_x(base, rows, out):
        @pl.loop(0, rows // 128)
        def _(tile):
            src = pl.ds(pl.multiple_of(base + tile * 128, 128), 128)
            out[0, block(tile, 128)] = mm_tn(place[:, src], tokens[...]).astype(BF)

    def build_dy(base, rows, out):
        @pl.loop(0, rows // 128)
        def _(tile):
            src = pl.ds(pl.multiple_of(base + tile * 128, 128), 128)
            value = mm_tn(place_hi[:, src], cot[...]) + mm_tn(place_lo[:, src], cot[...])
            out[1, block(tile, 128)] = value.astype(BF)

    def scatter(sem, src_of, dst_of):
        @pl.loop(1, n)
        def _(step):
            other = peer(lax.rem(step * 5, n))
            pltpu.make_async_remote_copy(
                src_ref=src_of(other),
                dst_ref=dst_of(me),
                send_sem=a2a_s.at[sem],
                recv_sem=a2a_r.at[sem],
                device_id={"expert": other},
                device_id_type=MESH,
            ).start()

    def landed(sem, ref):
        pltpu.make_async_copy(ref, ref, a2a_r.at[sem]).wait()

    def left_here(sem, ref):
        pltpu.make_async_copy(ref, ref, a2a_s.at[sem]).wait()

    all_p, all_m, peers = pl.ds(0, (n - 1) * dp), pl.ds(0, (n - 1) * dm), pl.ds(0, n - 1)

    def dispatch(sem, which, size, src, dst):
        scatter(sem, lambda d: src.at[which, block(d, size)], lambda m: dst.at[which, block(m, size)])
        dst[which, block(me, size)] = src[which, block(me, size)]

    make_place(0)
    build_x(0, rows_p, sx_p)
    pl.semaphore_wait(barrier, n + 1)
    dispatch(0, 0, dp, sx_p, rx_p)
    build_dy(0, rows_p, sx_p)
    dispatch(1, 1, dp, sx_p, rx_p)

    slot, is_src = jnp.int32(0), jnp.int32(0)
    for m in range(pairs):
        s, t = sources[m], targets[m]
        at_s, at_t = lax.shift_right_logical(s, 1) == me, lax.shift_right_logical(t, 1) == me
        slot = jnp.where(at_s, s & 1, jnp.where(at_t, t & 1, slot))
        is_src = jnp.where(at_s, 1, is_src)
    held = lax.broadcasted_iota(jnp.int32, marks.shape, 0)
    marks[...] = jnp.where(held == slot, 1 + is_src, 0)

    def fill_table(device, carry):
        partner = jnp.int32(0)
        for m in range(pairs):
            s, t = lax.shift_right_logical(sources[m], 1), lax.shift_right_logical(targets[m], 1)
            partner = jnp.where(s == device, t, jnp.where(t == device, s, partner))
        table[device] = partner
        return carry

    perm = jnp.zeros((8, neurons), jnp.int32)
    for m in range(pairs):
        s, t = lax.shift_right_logical(sources[m], 1), lax.shift_right_logical(targets[m], 1)
        mine = jnp.where((s == me) | (t == me), 1, 0)
        perm = perm + perm_ref[m : m + 1, :] * mine
    perm = perm[0:1, :]
    lane = lax.broadcasted_iota(jnp.int32, (1, half), 1)
    send_ids = jnp.where(is_src > 0, perm[:, :half], lane + tail)
    keep_ids = jnp.where(is_src > 0, perm[:, tail:], lane)

    def ordered(ids, span, out):
        units = ids[:, span.start : span.start + span.size]

        @pl.loop(0, neurons // 128)
        def _(tile):
            rows = lax.broadcasted_iota(jnp.int32, (128, span.size), 0) + tile * 128
            hot[block(tile, 128)] = jnp.where(rows == units, 1.0, 0.0).astype(BF)

        @pl.loop(0, 3)
        def _(q):
            out[q, :, span] = mm(weights[q, slot], hot[...]).astype(BF)

    def first_hop(i):
        scatter(2 + i, lambda d: w_send.at[:, block(d, piece), spans[i]], lambda m: w_mid[i].at[m])
        w_mid[i][me] = w_send[:, block(me, piece), spans[i]]

    def second_hop(first, then, mid, span, dst_of):
        landed(first, mid.at[peers])
        left_here(first, mid.at[peers])

        @pl.loop(0, n)
        def _(other):
            w_send[:, block(other, piece), span] = mid[table[other]]

        scatter(then, lambda d: w_send.at[:, block(d, piece), span], dst_of)

    def weight_hop(i):
        second_hop(2 + i, 5 + i, w_mid[i], spans[i], lambda m: w_got.at[:, block(m, piece), spans[i]])
        w_got[:, block(me, piece), spans[i]] = w_send[:, block(me, piece), spans[i]]

    for load in loads:
        load.wait()
    ordered(send_ids, spans[0], w_send)
    first_hop(0)
    make_place(1)
    make_place(2)
    build_x(rows_p, rows_m, sx_m)
    dispatch(8, 0, dm, sx_m, rx_m)

    lefts = (0, 0, 1)

    def product_p(q):
        def product(index):
            return mm(rx_p[lefts[q], block(index, ring_p.chunk), :], weights[q, 1 - slot])

        return product

    def product_m(i, q):
        def product(index):
            return mm(rx_m[lefts[q], block(index, blocks[i].chunk), :], w_keep[q, :, spans[i]])

        return product

    landed(0, rx_p.at[0, all_p])
    ring_p.start(0, product_p(0))
    ring_p.start(1, product_p(1))
    build_dy(rows_p, rows_m, sx_m)
    landed(1, rx_p.at[1, all_p])
    ring_p.start(2, product_p(2))
    ring_p.rest(0, product_p(0))
    ring_p.second(0)
    ring_p.rest(1, product_p(1))
    ring_p.second(1)
    lax.fori_loop(0, n, fill_table, 0)
    weight_hop(0)
    dispatch(9, 1, dm, sx_m, rx_m)
    ring_p.rest(2, product_p(2))
    ring_p.second(2)
    for i in range(1, BLOCKS):
        ordered(send_ids, spans[i], w_send)
        first_hop(i)
    for i in range(BLOCKS):
        ordered(keep_ids, spans[i], w_keep)

    def blend(i):
        landed(5 + i, w_got.at[:, pl.ds(0, (n - 1) * piece), spans[i]])

        @pl.loop(0, 3 * (width // 128))
        def _(tile):
            q, rows = lax.div(tile, width // 128), block(lax.rem(tile, width // 128), 128)
            both = w_keep[q, rows, spans[i]].astype(F32) + w_got[q, rows, spans[i]].astype(F32)
            w_keep[q, rows, spans[i]] = (0.5 * both).astype(BF)

    def gradient(left, full, rows, q, store):
        tile_n = 256

        @pl.loop(0, width // tile_n)
        def _(tile):
            right = full[q].reshape(rows, full.shape[3])
            store(tile, mm_tn(left[:, block(tile, tile_n)], right).astype(BF))

    def grads_p(q, target):
        def store(tile, value):
            part_p[target, pl.ds(tile * 2, 2)] = value.reshape(2, 128, neurons)

        gradient(rx_p.at[1 if q == 0 else 0], full_p, rows_p, q, store)
        pltpu.make_async_copy(part_p.at[target], out_p[target], out_s.at[target]).start()

    halves = pl.ds(0, 2)
    jobs = []

    def put(src, dst):
        copy = pltpu.make_async_copy(src, dst, out_s.at[3 + len(jobs)])
        copy.start()
        jobs.append(copy)

    def grads_m(i, q, target):
        part = blocks[i].part

        def store(tile, value):
            part[target, tile] = value

        gradient(rx_m.at[1 if q == 0 else 0], blocks[i].full, rows_m, q, store)

    def grad_hop(i):
        part, mid = blocks[i].part, g_mid[i]
        size = pl.ds(cut[i], cols - cut[i])

        def src(d):
            return part.at[:, lax.div(d, n // 2), block(lax.rem(d, n // 2), piece), size]

        scatter(10 + i, src, lambda m: mid.at[m])
        mid[me] = part[:, lax.div(me, n // 2), block(lax.rem(me, n // 2), piece), size]
        for q in range(3):
            put(part.at[q, halves], out_m[q].at[:, :, spans[i]])

    def back_hop(i):
        far, size = g_far[i], pl.ds(spans[i].start, cols - cut[i])
        left_here(5 + i, w_mid[i].at[peers])

        def dst(m):
            return far.at[:, lax.div(m, n // 2), block(lax.rem(m, n // 2), piece), :]

        second_hop(10 + i, 13 + i, g_mid[i], size, dst)
        rows = block(lax.rem(me, n // 2), piece)
        far[:, lax.div(me, n // 2), rows, :] = w_send[:, block(me, piece), size]

    unit = lax.broadcasted_iota(jnp.int32, (1, cols), 1)
    cover = jnp.where((unit < skip) & (is_src > 0), 0.0, 1.0).astype(F32)

    def mix_outputs():
        landed(16, back_p.at[all_p])
        landed(17, back_m.at[all_m])
        span_p, span_m = pl.ds(0, rows_p), pl.ds(rows_p, rows_m)
        total = mm(place_hi[:, span_p], back_p[...]) + mm(place_lo[:, span_p], back_p[...])
        total += mm(place_hi[:, span_m], back_m[...]) + mm(place_lo[:, span_m], back_m[...])
        mixed[...] = total.astype(BF)

    def enter(i):
        blend(i)
        for q in range(3):
            blocks[i].start(q, product_m(i, q))

    def rest(i):
        for q in range(3):
            blocks[i].rest(q, product_m(i, q))

    def seconds(i):
        for q in range(3):
            blocks[i].second(q)

    def publish(i):
        blocks[i].acts(cover if cut[i] else None)
        for q in range(3):
            blocks[i].publish(q)

    def forwards(i):
        for q in range(3):
            blocks[i].forward(q)

    def leave(i):
        blocks[i].sent((0, 1, 2, 3))
        for q, target in ((0, 2), (1, 0), (2, 1)):
            blocks[i].arrived(q)
            grads_m(i, q, target)
        grad_hop(i)

    def outputs_p():
        ring_p.arrived(0)
        left_here(0, sx_p.at[0, all_p])
        for index in range(N_HID):
            rows = pl.ds(index * ring_p.chunk, ring_p.chunk)
            sx_p[0, rows] = mm_nt(full_p[0, index], weights[2, 1 - slot]).astype(BF)
        scatter(16, lambda d: sx_p.at[0, block(d, dp)], lambda m: back_p.at[block(m, dp)])
        back_p[block(me, dp)] = sx_p[0, block(me, dp)]

    def outputs_m():
        for i in range(BLOCKS):
            blocks[i].arrived(0)
        left_here(8, sx_m.at[0, all_m])
        for index in range(N_HID):
            rows = pl.ds(index * blocks[0].chunk, blocks[0].chunk)
            value = mm_nt(blocks[0].full[0, index], w_keep[2, :, spans[0]])
            for i in range(1, BLOCKS):
                value += mm_nt(blocks[i].full[0, index], w_keep[2, :, spans[i]])
            sx_m[0, rows] = value.astype(BF)
        scatter(17, lambda d: sx_m.at[0, block(d, dm)], lambda m: back_m.at[block(m, dm)])
        back_m[block(me, dm)] = sx_m[0, block(me, dm)]

    landed(8, rx_m.at[0, all_m])
    blend(0)
    blocks[0].start(0, product_m(0, 0))
    blocks[0].start(1, product_m(0, 1))
    ring_p.acts(None)
    ring_p.publish(0)
    blocks[0].rest(0, product_m(0, 0))
    blocks[0].second(0)
    blocks[0].rest(1, product_m(0, 1))
    blocks[0].second(1)
    landed(9, rx_m.at[1, all_m])
    blocks[0].start(2, product_m(0, 2))
    blocks[0].rest(2, product_m(0, 2))
    weight_hop(1)
    blocks[0].second(2)
    ring_p.forward(0)
    publish(0)
    weight_hop(2)
    enter(1)
    rest(1)
    forwards(0)
    outputs_p()
    enter(2)
    seconds(1)
    rest(2)
    leave(0)
    publish(1)
    seconds(2)
    back_hop(0)
    forwards(1)
    publish(2)
    leave(1)
    forwards(2)
    ring_p.publish(1)
    ring_p.publish(2)
    ring_p.sent((0, 1, 2, 3))
    leave(2)
    back_hop(1)
    outputs_m()
    ring_p.forward(1)
    back_hop(2)
    ring_p.forward(2)
    grads_p(0, 2)
    ring_p.arrived(1)
    grads_p(1, 0)
    ring_p.arrived(2)
    grads_p(2, 1)

    for i in range(BLOCKS):
        if i == BLOCKS - 1:
            mix_outputs()
        landed(13 + i, g_mid[i].at[peers])
        for q in range(3):
            put(g_far[i].at[q], out_m[q].at[:, :, pl.ds(tail + spans[i].start + cut[i], cols - cut[i])])

    left_here(1, sx_p.at[1, all_p])
    left_here(9, sx_m.at[1, all_m])
    left_here(16, sx_p.at[0, all_p])
    left_here(17, sx_m.at[0, all_m])
    for i in range(BLOCKS):
        left_here(13 + i, g_mid[i].at[peers])
    for ring in rings:
        ring.sent((4, 5, 6, 7))
    for q in range(3):
        pltpu.make_async_copy(part_p.at[q], out_p[q], out_s.at[q]).wait()
    for job in jobs:
        job.wait()


def mega(sources, targets, perm, routing, route_w, tokens, cot, gate, up, down, n, depth):
    width, neurons = gate.shape[1], gate.shape[2]
    half = -(-neurons // 256) * 128
    far = neurons - half
    cols = half // BLOCKS
    fars = [cols] * (BLOCKS - 1) + [far - (BLOCKS - 1) * cols]
    rows_p, rows_m = n * depth, 2 * n * depth
    piece = width // n
    cp, cm = rows_p // N_HID, rows_m // N_HID
    vmem = pl.BlockSpec(memory_space=pltpu.VMEM)
    smem = pl.BlockSpec(memory_space=pltpu.SMEM)
    hbm = pl.BlockSpec(memory_space=pl.ANY)

    def ring(chunk, cols):
        return [
            pltpu.VMEM((3, N_HID, chunk, cols), BF),
            pltpu.VMEM((3, chunk // 2, cols), BF),
            pltpu.VMEM((3, chunk // 2, cols), BF),
            pltpu.VMEM((3, chunk, cols), BF),
            pltpu.VMEM((3, chunk, cols), BF),
            pltpu.VMEM((3, N_HID, chunk, cols), BF),
        ]

    return pl.pallas_call(
        mega_kernel,
        out_shape=(
            jax.ShapeDtypeStruct(tokens.shape, BF),
            jax.ShapeDtypeStruct((gate.shape[0], neurons), jnp.int32),
            *[jax.ShapeDtypeStruct((width // 128, 128, neurons), BF)] * 3,
            *[jax.ShapeDtypeStruct((2, width // 2, neurons), BF)] * 3,
        ),
        in_specs=[smem] * 2 + [vmem] * 5 + [hbm] * 3,
        out_specs=(vmem, vmem, *[hbm] * 6),
        scratch_shapes=[
            pltpu.SMEM((n,), jnp.int32),
            pltpu.VMEM((3, *gate.shape), BF),
            pltpu.VMEM((2, 8, tokens.shape[0]), F32),
            *[pltpu.VMEM((tokens.shape[0], rows_p + rows_m), BF)] * 3,
            pltpu.VMEM((neurons, cols), BF),
            pltpu.VMEM((2, rows_p, width), BF),
            pltpu.VMEM((2, rows_m, width), BF),
            pltpu.VMEM((2, rows_p, width), BF),
            pltpu.VMEM((2, rows_m, width), BF),
            *[pltpu.VMEM((3, width, half), BF)] * 3,
            pltpu.VMEM((rows_p, width), BF),
            pltpu.VMEM((rows_m, width), BF),
            *[pltpu.VMEM((n, 3, piece, cols), BF)] * BLOCKS,
            *[pltpu.VMEM((n, 3, piece, size), BF) for size in fars],
            *[pltpu.VMEM((3, 2, width // 2, size), BF) for size in fars],
            *ring(cp, neurons),
            *(ring(cm, cols) * BLOCKS),
            pltpu.SemaphoreType.DMA((2 + 2 * BLOCKS, 8, 3)),
            pltpu.SemaphoreType.DMA((18,)),
            pltpu.SemaphoreType.DMA((18,)),
            pltpu.SemaphoreType.DMA((3,)),
            pltpu.SemaphoreType.DMA((3 + 6 * BLOCKS,)),
        ],
        compiler_params=pltpu.CompilerParams(
            collective_id=0, has_side_effects=True, vmem_limit_bytes=67_043_328
        ),
    )(sources, targets, perm, routing, route_w, tokens, cot, gate, up, down)


def shards(
    tokens,
    cotangent,
    gate_weight,
    up_weight,
    down_weight,
    routing,
    route_weight,
    merge_source,
    merge_target,
    neuron_perm,
):
    devices_n = lax.axis_size("expert")
    exp_local, width, neurons = gate_weight.shape
    tok_local, top_count = routing.shape
    depth = max(2, tok_local * top_count * 4 // (3 * exp_local * devices_n))
    mixed, marks, *grads = mega(
        merge_source,
        merge_target,
        neuron_perm,
        routing.T,
        route_weight.T,
        tokens,
        cotangent,
        gate_weight,
        up_weight,
        down_weight,
        devices_n,
        depth,
    )
    marks = marks[:, None, :]

    def final(q):
        plain = grads[q].reshape(1, width, neurons)
        merged = grads[3 + q].reshape(1, width, neurons)
        rest = jnp.where(marks == 2, jnp.zeros((), BF), plain)
        return jnp.where(marks == 1, merged, rest)

    return (mixed, final(0), final(1), final(2))


def solution(mesh):
    placed = (
        P("expert", "hidden"),
        P("expert", "hidden"),
        P("expert", "hidden", None),
        P("expert", "hidden", None),
        P("expert", "hidden", None),
        P("expert", None),
        P("expert", None),
        P(),
        P(),
        P(),
    )
    return jax.shard_map(
        shards,
        mesh=mesh,
        in_specs=placed,
        out_specs=(
            P("expert", "hidden"),
            P("expert", "hidden", None),
            P("expert", "hidden", None),
            P("expert", "hidden", None),
        ),
        check_vma=False,
    )
```
